32 devices in a mesh: groups: 2 (over x), slab: 16 (over z, y, core).
Axes of the slice: x: 2, y: 2, z: 4, core: 2. Of those that a mesh axis runs over, the one named last changes fastest.
Arguments:
- wavefields: float32 [2, 4, 4, 2048, 512], P(None, None, 'groups', 'slab'), parts along dimension 2, may hold values from -6 to 6
- courant: float32 [2048, 512], P('slab'), may hold values from 0.04 to 0.16
- epsilon: float32 [2048, 512], P('slab'), may hold values from 0.1 to 0.3
- anisotropy_delta: float32 [2048, 512], P('slab'), may hold values from 0 to 0.1
- tilt_angle: float32 [2048, 512], P('slab'), may hold values from -3.140625 to 3.140625
- loc_patch: int32 [256], replicated, may hold values from 0 to 63, as said below
- slab_counts: int32 [16], replicated, may hold values from 3 to 4
- angle_table: int32 [64], replicated, may hold values from -48 to 47
Outputs:
- gathers: float32 [512, 4096], P(('groups', 'slab')), parts along dimension 0
The draws below stay inside these ranges and needn't reach their ends.
There are 2 independent parts, one for each index of `groups`. The reference program is written for one: setup_inputs(seed, part) draws one part's arguments, and reference() takes and returns one part's arrays. A program takes and returns all parts, laid end to end along the dimension named above; an argument that names none is the same for every part. Nothing has to cross between parts.
Inputs may be any that keep to these rules, and one draw needn't show every extreme that they name: `loc_patch`: location g names a patch id slab * 4 + column block; locations g of one owner are the 16 rows of an aligned block. Within one block no slab is named by more than 2 locations, and some slab is named by exactly 2 in every block.
All inputs are finite; a program needn't handle non-finite values.
Results may differ from the reference program's by a relative error of at most 0.0055.
Values may be sent and summed in bfloat16 or wider, within the bound.
A program may use at most 128 MiB of HBM per device.

```python
import math
import jax
import jax.numpy as jnp
from jax import lax

PATCH = 128
ANG = 64
SHOTS = 2
STEPS = 2
NX = 512
BINS = 64
NZ = 2048
LOC_DEV = 16
LOC = 256
N_SLAB = 16


def draw_loc_patch(key, part):
    keys = jax.random.split(jax.random.fold_in(key, 7), 3)
    blocks = LOC // LOC_DEV
    half_count = LOC_DEV // 2
    slab_ids = jnp.arange(LOC_DEV, dtype=jnp.int32)
    scores = jax.random.randint(keys[0], (blocks, LOC_DEV), 0, 64, dtype=jnp.int32) + 32 * (slab_ids < LOC_DEV // 4).astype(jnp.int32)[None, :]
    ranked = scores * LOC_DEV + slab_ids[None, :]
    ordering = jnp.argsort(-ranked, axis=1).astype(jnp.int32)
    flips = (jax.random.randint(keys[1], (blocks, LOC_DEV), 0, 4, dtype=jnp.int32) == 0).astype(jnp.int32)
    flips = flips.at[:, 0:2].set(0)
    position = jnp.arange(LOC_DEV, dtype=jnp.int32)
    chosen_rank = position[None, :] // 2 + half_count * flips
    slabs = jnp.take_along_axis(ordering, chosen_rank, axis=1)
    columns = jax.random.randint(keys[2], (blocks, LOC_DEV), 0, NX // PATCH, dtype=jnp.int32)
    return (slabs * (NX // PATCH) + columns).reshape(LOC).astype(jnp.int32)


def place_ends(array, own_key, least, top_value):
    longest = array.shape.index(max(array.shape))
    spots = []
    for shift in (0, 1):
        where = [jax.random.randint(jax.random.fold_in(own_key, axis), (), 0, length) for axis, length in enumerate(array.shape)]
        where[longest] = (where[longest] + shift) % array.shape[longest]
        spots.append(tuple(where))
    return array.at[spots[0]].set(least).at[spots[1]].set(top_value)


def block_scale(own_key, shape, shards, low, top_value):
    def one(dim, parts):
        heights = jax.random.uniform(jax.random.fold_in(jax.random.fold_in(own_key, 6), dim), (parts,), jnp.float32, low / len(shards), top_value / len(shards))
        return jnp.repeat(jnp.exp(heights), shape[dim] // parts).reshape((-1,) + (1,) * (len(shape) - dim - 1))

    factor_of = one(*shards[0])
    for cut in shards[1:]:
        factor_of = factor_of * one(*cut)
    return factor_of


def noise(stream_key, shape, deviation, reach, shards=(), kind=jnp.bfloat16):
    level = block_scale(stream_key, shape, shards, -0.22, 0.18) if shards else 1.0
    array = jax.random.normal(stream_key, shape, jnp.float32) * deviation * level
    return jnp.minimum(jnp.maximum(array, -reach), reach).astype(kind)


def setup_inputs(seed: int = 0, part: int = 0) -> dict:
    key_of = jax.random.split(jax.random.key(seed), 9)
    part_splits = jax.random.split(jax.random.fold_in(key_of[8], part), 9)
    wavefields = noise(part_splits[0], (2, 4, SHOTS, NZ, NX), 1.0, 6.0, ((3, 16),), jnp.float32)
    courant = jnp.clip(0.04 + 0.12 * jax.random.uniform(key_of[1], (NZ, NX), jnp.float32) ** block_scale(key_of[1], (NZ, NX), ((0, 16),), -0.2, 0.2), 0.04, 0.16)
    epsilon = jnp.clip(0.1 + 0.20000001043081284 * jax.random.uniform(key_of[2], (NZ, NX), jnp.float32) ** block_scale(key_of[2], (NZ, NX), ((0, 16),), -0.2, 0.2), 0.1, 0.3)
    anisotropy_delta = jnp.clip(0.1 * jax.random.uniform(key_of[3], (NZ, NX), jnp.float32) ** block_scale(key_of[3], (NZ, NX), ((0, 16),), -0.2, 0.2), 0.0, 0.1)
    tilt_angle = jnp.clip(jax.random.uniform(key_of[4], (NZ, NX), jnp.float32, -3.140625, 3.140625), -3.140625, 3.140625)
    loc_patch = draw_loc_patch(jax.random.fold_in(key_of[8], 71), part)
    slab_counts = place_ends(jax.random.randint(key_of[6], (N_SLAB,), NX // PATCH - 1, NX // PATCH + 1), jax.random.fold_in(key_of[6], 1), NX // PATCH - 1, (NX // PATCH + 1) - 1).astype(jnp.int32)
    angle_table = place_ends(jax.random.randint(key_of[7], (ANG,), -48, 48), jax.random.fold_in(key_of[7], 1), -48, 47).astype(jnp.int32)
    return {"wavefields": wavefields, "courant": courant, "epsilon": epsilon, "anisotropy_delta": anisotropy_delta, "tilt_angle": tilt_angle, "loc_patch": loc_patch, "slab_counts": slab_counts, "angle_table": angle_table}


SECOND_TERMS = (-205.0 / 72.0, 8.0 / 5.0, -1.0 / 5.0, 8.0 / 315.0, -1.0 / 560.0)
FIRST_TERMS = (4.0 / 5.0, -1.0 / 5.0, 4.0 / 105.0, -1.0 / 280.0)

def pad_columns(field):
    widths = [(0, 0)] * (field.ndim - 1) + [(4, 4)]
    return jnp.pad(field, widths)

def derivatives(field):
    row_count = field.shape[-2] - 8
    column_count = field.shape[-1]
    middle = field[..., 4:4 + row_count, :]
    beside = pad_columns(middle)
    second_z = SECOND_TERMS[0] * middle
    second_x = SECOND_TERMS[0] * middle
    first_z = jnp.zeros_like(middle)
    for offset in range(1, 5):
        upper_rows = field[..., 4 + offset:4 + offset + row_count, :]
        lower_rows = field[..., 4 - offset:4 - offset + row_count, :]
        second_z = second_z + SECOND_TERMS[offset] * (upper_rows + lower_rows)
        first_z = first_z + FIRST_TERMS[offset - 1] * (upper_rows - lower_rows)
        second_x = second_x + SECOND_TERMS[offset] * (beside[..., 4 + offset:4 + offset + column_count] + beside[..., 4 - offset:4 - offset + column_count])
    spread = pad_columns(first_z)
    mixed_term = jnp.zeros_like(middle)
    for offset in range(1, 5):
        mixed_term = mixed_term + FIRST_TERMS[offset - 1] * (spread[..., 4 + offset:4 + offset + column_count] - spread[..., 4 - offset:4 - offset + column_count])
    return (second_x, second_z, mixed_term)

def advance(current, previous, courant, epsilon, anisotropy_delta, tilt_angle):
    second_x, second_z, mixed_term = derivatives(current)
    sine_tilt = jnp.sin(tilt_angle)
    cosine = jnp.cos(tilt_angle)
    along_axis = sine_tilt * sine_tilt * second_x + cosine * cosine * second_z + 2.0 * sine_tilt * cosine * mixed_term
    across = second_x + second_z - along_axis
    root_delta = jnp.sqrt(1.0 + 2.0 * anisotropy_delta)
    push_pressure = (1.0 + 2.0 * epsilon) * across[:, 0] + root_delta * along_axis[:, 1]
    push_other = root_delta * across[:, 0] + along_axis[:, 1]
    middle = current[..., 4:-4, :]
    return 2.0 * middle - previous + courant * jnp.stack([push_pressure, push_other], axis=1)

def depth_table(patch, bins):
    wavenumber = jnp.arange(bins, dtype=jnp.int32)[:, None]
    depth_index = jnp.arange(patch, dtype=jnp.int32)[None, :]
    phase = 2.0 * math.pi / patch * jnp.mod(wavenumber * depth_index, patch).astype(jnp.float32)
    scale = 1.0 / math.sqrt(patch)
    return jnp.concatenate([jnp.cos(phase), -jnp.sin(phase)], axis=0) * scale

def slant_table(angle_table, patch, bins):
    wavenumber = jnp.arange(bins, dtype=jnp.int32)[:, None, None]
    lateral = jnp.arange(patch, dtype=jnp.int32)[None, None, :]
    slopes = angle_table.astype(jnp.int32)[None, :, None]
    modulus = 16 * patch
    phase = 2.0 * math.pi / modulus * jnp.mod(wavenumber * slopes * lateral, modulus).astype(jnp.float32)
    scale = 1.0 / math.sqrt(patch)
    real_part = jnp.cos(phase) * scale
    imag_part = -jnp.sin(phase) * scale
    upper_half = jnp.stack([real_part, -imag_part], axis=2)
    lower_half = jnp.stack([imag_part, real_part], axis=2)
    return jnp.concatenate([upper_half, lower_half], axis=1).astype(jnp.bfloat16)

def correlate(stacked, angles):
    shaped = stacked.reshape(stacked.shape[:-1] + (2, angles))
    product = shaped[..., 0, :, :, :, :] * shaped[..., 1, :, :, :, :]
    summed = lax.optimization_barrier(jnp.sum(product, axis=(-4, -2)))
    return summed.reshape(summed.shape[:-2] + (summed.shape[-2] * angles,))

def reference(wavefields, courant, epsilon, anisotropy_delta, tilt_angle, loc_patch, slab_counts, angle_table):
    states = jnp.transpose(wavefields, (0, 2, 1, 3, 4)).reshape(2 * SHOTS, 4, NZ, NX)

    def evolve(state):
        current = state[None, 0:2]
        previous = state[None, 2:4]
        for iteration in range(STEPS):
            extended = jnp.pad(current, ((0, 0), (0, 0), (4, 4), (0, 0)))
            current, previous = (advance(extended, previous, courant, epsilon, anisotropy_delta, tilt_angle), current)
        return current[0, 0]
    pressure = lax.map(evolve, states).reshape(2, SHOTS, N_SLAB, PATCH, NX)
    table = depth_table(PATCH, BINS)
    spectra = jnp.einsum('qz,fsbzx->fsbqx', table, pressure, precision=lax.Precision.HIGHEST).astype(jnp.bfloat16)
    spectra = spectra.reshape(2, SHOTS, N_SLAB, 2, BINS, NX // PATCH, PATCH)
    slant = slant_table(angle_table, PATCH, BINS).astype(jnp.float32)

    def image_slab(slab_number):
        piece = lax.dynamic_index_in_dim(spectra, slab_number, 2, keepdims=False).astype(jnp.float32)
        stacked = jnp.einsum('kirx,fsrkpx->pfski', slant, piece, precision=lax.Precision.HIGHEST)
        return correlate(stacked, ANG)
    images = lax.map(image_slab, jnp.arange(N_SLAB, dtype=jnp.int32))
    alive = (jnp.arange(NX // PATCH, dtype=jnp.int32)[None, :] < slab_counts[:, None]).astype(jnp.float32)
    images = (images * alive[:, :, None]).reshape(N_SLAB * (NX // PATCH), BINS * ANG)
    return jnp.take(images, loc_patch, axis=0)
```

```python
import functools
import math

import jax
import jax.numpy as jnp
from jax import lax
from jax.experimental import pallas as pl
from jax.experimental.pallas import tpu as pltpu
from jax.sharding import PartitionSpec as P

MESH = pl.DeviceIdType.MESH
PAD = 16
REACH = 4
SECOND_TERMS = (-205.0 / 72.0, 8.0 / 5.0, -1.0 / 5.0, 8.0 / 315.0, -1.0 / 560.0)
FIRST_TERMS = (4.0 / 5.0, -1.0 / 5.0, 4.0 / 105.0, -1.0 / 280.0)


def sincos_turns(u):
    quarter = jnp.round(4.0 * u)
    theta = (u - 0.25 * quarter) * (2.0 * math.pi)
    sq = theta * theta
    sine = theta + theta * sq * (
        -1.0 / 6 + sq * (1.0 / 120 + sq * (-1.0 / 5040 + sq * (1.0 / 362880)))
    )
    cosine = 1.0 + sq * (-0.5 + sq * (1.0 / 24 + sq * (-1.0 / 720 + sq * (1.0 / 40320))))
    q = quarter.astype(jnp.int32)
    odd = (q & 1) == 1
    s = jnp.where(odd, cosine, sine)
    c = jnp.where(odd, sine, cosine)
    s = jnp.where((q & 2) == 2, -s, s)
    c = jnp.where(((q + 1) & 2) == 2, -c, c)
    return s, c


def band(distance, second):
    out = jnp.zeros(distance.shape, jnp.float32)
    if second:
        out = jnp.where(distance == 0, SECOND_TERMS[0], out)
    for offset in range(1, REACH + 1):
        weight = SECOND_TERMS[offset] if second else FIRST_TERMS[offset - 1]
        out = jnp.where(distance == offset, weight, out)
        out = jnp.where(distance == -offset, weight if second else -weight, out)
    return out


def iota(shape, dim):
    return lax.broadcasted_iota(jnp.int32, shape, dim)


def dot(a, b):
    return jnp.dot(a, b, preferred_element_type=jnp.float32)


def kernel(
    n,
    wav,
    courant,
    epsilon,
    delta,
    tilt,
    loc,
    counts,
    angle,
    out,
    state,
    c_in,
    e_in,
    d_in,
    t_in,
    ext1,
    ext2,
    ca,
    cb,
    cd,
    ce,
    cr,
    zmat,
    x2mat,
    x1mat,
    cos1,
    sin1,
    cos2,
    sin2,
    yre,
    yim,
    img,
    gath,
    in_sem,
    halo_send,
    halo_recv,
    ag_send,
    ag_recv,
):
    me = lax.axis_index("slab")
    _, _, shots, rows, cols = wav.shape
    patches = cols // rows
    bins = rows // 2
    angles = angle.shape[0]
    pairs = 2 * shots
    group = 2 * shots * patches
    half = group // 2
    block = out.shape[0]
    chunks = bins * angles // 128
    split = 8

    loads = []
    for j, (src, dst) in enumerate(
        (
            (wav.at[:, 0:2], state.at[:, 0:2]),
            (tilt, t_in),
            (epsilon, e_in),
            (delta, d_in),
            (courant, c_in),
            (wav.at[:, 2:4], state.at[:, 2:4]),
        )
    ):
        copy = pltpu.make_async_copy(src, dst, in_sem.at[j])
        copy.start()
        loads.append(copy)

    zero = jnp.zeros((2 * pairs, PAD, cols), jnp.bfloat16)
    for ext in (ext1, ext2):
        ext[:, 0:PAD, :] = zero
        ext[:, PAD + rows :, :] = zero

    barrier = pltpu.get_barrier_semaphore()
    for d in range(1, n):
        pl.semaphore_signal(
            barrier, inc=1, device_id={"slab": lax.rem(me + d, n)}, device_id_type=MESH
        )

    tall = rows + 2 * PAD
    reach = iota((rows, tall), 1) - PAD - iota((rows, tall), 0)
    zmat[0:rows] = band(reach, True).astype(jnp.bfloat16)
    zmat[rows:] = band(reach, False).astype(jnp.bfloat16)
    wide = iota((cols, cols), 0) - iota((cols, cols), 1)
    x2mat[...] = band(wide, True).astype(jnp.bfloat16)
    x1mat[...] = band(wide, False).astype(jnp.bfloat16)

    lanes = 2 * angles
    modulus = 16 * rows
    lane = iota((1, lanes), 1)
    slope = jnp.zeros((1, lanes), jnp.int32)
    for a in range(angles):
        slope = jnp.where(lane % angles == a, angle[a], slope)
    step = slope * iota((rows, lanes), 0)
    turn = jnp.where(iota((rows, lanes), 1) >= angles, modulus // 4, 0)
    scale = 1.0 / math.sqrt(rows)

    def phases(k, carry):
        j = jnp.bitwise_and(k * split * step, modulus - 1)
        s, c = sincos_turns(j.astype(jnp.float32) * (1.0 / modulus))
        cos1[k] = c
        sin1[k] = s
        j = jnp.bitwise_and(k * step + turn, modulus - 1)
        s, c = sincos_turns(j.astype(jnp.float32) * (1.0 / modulus))
        cos2[k] = c * scale
        sin2[k] = s * scale
        return carry

    lax.fori_loop(0, split, phases, 0)

    pl.semaphore_wait(barrier, n - 1)
    loads[0].wait()

    up = jnp.maximum(me - 1, 0)
    down = jnp.minimum(me + 1, n - 1)

    def halo(ext, step, i, upward):
        first = pl.ds(2 * i, 2)
        if upward:
            src = ext.at[first, PAD : 2 * PAD, :]
            dst = ext.at[first, PAD + rows : 2 * PAD + rows, :]
        else:
            src = ext.at[first, rows : PAD + rows, :]
            dst = ext.at[first, 0:PAD, :]
        way = 0 if upward else 1
        return pltpu.make_async_remote_copy(
            src_ref=src,
            dst_ref=dst,
            send_sem=halo_send.at[step, way, i],
            recv_sem=halo_recv.at[step, way, i],
            device_id={"slab": up if upward else down},
            device_id_type=MESH,
        )

    def send(ext, step, i):
        @pl.when(me > 0)
        def _():
            halo(ext, step, i, True).start()

        @pl.when(me < n - 1)
        def _():
            halo(ext, step, i, False).start()

    def receive(ext, step, i):
        @pl.when(me > 0)
        def _():
            halo(ext, step, i, False).wait_recv()

        @pl.when(me < n - 1)
        def _():
            halo(ext, step, i, True).wait_recv()

    def finish(ext, step, i):
        @pl.when(me > 0)
        def _():
            halo(ext, step, i, True).wait_send()

        @pl.when(me < n - 1)
        def _():
            halo(ext, step, i, False).wait_send()

    def convert(i, carry):
        f, s = i // shots, i % shots
        for w in range(2):
            ext1[2 * i + w, PAD : PAD + rows, :] = state[f, w, s].astype(jnp.bfloat16)
        send(ext1, 0, i)
        return carry

    lax.fori_loop(0, pairs, convert, 0)

    for copy in loads[1:5]:
        copy.wait()
    sine, cosine = sincos_turns(t_in[...] * (1.0 / math.pi))
    ca[...] = 0.5 - 0.5 * cosine
    cb[...] = 0.5 + 0.5 * cosine
    cd[...] = sine
    ce[...] = c_in[...] * (1.0 + 2.0 * e_in[...])
    cr[...] = c_in[...] * jnp.sqrt(1.0 + 2.0 * d_in[...])
    loads[5].wait()

    def terms(ext, field):
        z = dot(zmat[...], ext[field])
        xx = dot(ext[field, PAD : PAD + rows, :], x2mat[...])
        xz = dot(z[rows:].astype(jnp.bfloat16), x1mat[...])
        return xx, z[:rows], xz

    def first(i, carry):
        f, s = i // shots, i % shots
        receive(ext1, 0, i)
        xx, zz, xz = terms(ext1, 2 * i)
        across = cb[...] * xx + ca[...] * zz - cd[...] * xz
        xx, zz, xz = terms(ext1, 2 * i + 1)
        along = ca[...] * xx + cb[...] * zz + cd[...] * xz
        p = 2.0 * state[f, 0, s] - state[f, 2, s] + ce[...] * across + cr[...] * along
        q = 2.0 * state[f, 1, s] - state[f, 3, s] + cr[...] * across + c_in[...] * along
        state[f, 2, s] = p
        ext2[2 * i, PAD : PAD + rows, :] = p.astype(jnp.bfloat16)
        ext2[2 * i + 1, PAD : PAD + rows, :] = q.astype(jnp.bfloat16)
        send(ext2, 1, i)
        return carry

    lax.fori_loop(0, pairs, first, 0)

    kk = iota((rows, rows), 0)
    zz_ = iota((rows, rows), 1)
    turns = jnp.bitwise_and(jnp.where(kk >= bins, kk - bins, kk) * zz_, rows - 1)
    s_t, c_t = sincos_turns(turns.astype(jnp.float32) * (1.0 / rows))
    table = (jnp.where(kk >= bins, -s_t, c_t) * scale).astype(jnp.bfloat16)

    for i in range(pairs):
        f, s = i // shots, i % shots
        receive(ext2, 1, i)
        xx, zz, xz = terms(ext2, 2 * i)
        across = cb[...] * xx + ca[...] * zz - cd[...] * xz
        xx, zz, xz = terms(ext2, 2 * i + 1)
        along = ca[...] * xx + cb[...] * zz + cd[...] * xz
        p = 2.0 * state[f, 2, s] - state[f, 0, s] + ce[...] * across + cr[...] * along
        spectrum = dot(table, p.astype(jnp.bfloat16))
        for m in range(patches):
            part = spectrum[:, m * rows : (m + 1) * rows]
            slot = i * patches + m
            yre[pl.ds(slot, bins, stride=group), :] = part[:bins]
            yim[pl.ds(slot, bins, stride=group), :] = part[bins:]

    def stack(k):
        k1, k2 = k // split, k % split
        c1, s1, c2, s2 = cos1[k1], sin1[k1], cos2[k2], sin2[k2]
        weights = jnp.concatenate([c1 * c2 - s1 * s2, s1 * c2 + c1 * s2], axis=0)
        at = pl.ds(pl.multiple_of(k * group, group), group)
        data = jnp.concatenate([yre[at, :], yim[at, :]], axis=1)
        st = dot(data.astype(jnp.bfloat16), weights.astype(jnp.bfloat16))
        prod = st[:half] * st[half:]
        total = prod[:patches]
        for shot in range(1, shots):
            total = total + prod[shot * patches : (shot + 1) * patches]
        return total + pltpu.roll(total, angles, 1)

    side = iota((patches, lanes), 1)

    def images(t, carry):
        both = jnp.where(side < angles, stack(2 * t), stack(2 * t + 1))
        img[pl.ds(t, patches, stride=chunks), :] = both
        return carry

    lax.fori_loop(0, chunks, images, 0)

    live = iota((patches, chunks, lanes), 0) < counts[me]
    own = jnp.where(live, img[...].reshape(patches, chunks, lanes), 0.0)
    gath[pl.ds(me * patches, patches)] = own.astype(jnp.bfloat16)

    high = n // 4
    h, m, l = me // 4, (me // 2) % 2, me % 2
    sent = []

    def ident(a, b, c):
        return a * 4 + b * 2 + c

    def pass_on(b, target):
        at = gath.at[pl.ds(b * patches, patches)]
        copy = pltpu.make_async_remote_copy(
            src_ref=at,
            dst_ref=at,
            send_sem=ag_send.at[len(sent)],
            recv_sem=ag_recv.at[b],
            device_id={"slab": target},
            device_id_type=MESH,
        )
        copy.start()
        sent.append(copy)

    def arrive(b):
        at = gath.at[pl.ds(b * patches, patches)]
        pltpu.make_async_remote_copy(
            src_ref=at,
            dst_ref=at,
            send_sem=ag_send.at[0],
            recv_sem=ag_recv.at[b],
            device_id={"slab": ident(h, m, 1 - l)},
            device_id_type=MESH,
        ).wait_recv()

    mid, low = ident(h, 1 - m, l), ident(h, m, 1 - l)
    for d in range(1, high):
        pass_on(me, ident(lax.rem(h + d, high), m, l))
    pass_on(me, mid)
    pass_on(me, low)
    for d in range(1, high):
        b = ident(lax.rem(h + high - d, high), m, l)
        arrive(b)
        pass_on(b, mid)
        pass_on(b, low)
    for d in range(high):
        b = ident(lax.rem(h + high - d, high), 1 - m, l)
        arrive(b)
        pass_on(b, low)
    for d in range(high):
        a = lax.rem(h + high - d, high)
        arrive(ident(a, m, 1 - l))
        arrive(ident(a, 1 - m, 1 - l))

    for g in range(block):
        out[g] = gath[loc[me * block + g]].astype(jnp.float32)

    for copy in sent:
        copy.wait_send()
    for i in range(pairs):
        finish(ext1, 0, i)
        finish(ext2, 1, i)


def per_device(
    n, wavefields, courant, epsilon, anisotropy_delta, tilt_angle, loc_patch, slab_counts, angle_table
):
    _, _, shots, rows, cols = wavefields.shape
    patches = cols // rows
    bins = rows // 2
    angles = angle_table.shape[0]
    block = loc_patch.shape[0] // n
    chunks = bins * angles // 128
    pairs = 2 * shots
    group = pairs * patches
    high = n // 4
    f32, bf16 = jnp.float32, jnp.bfloat16
    vm = pltpu.VMEM
    plane = vm((rows, cols), f32)
    table = vm((8, rows, 2 * angles), f32)
    ext = vm((2 * pairs, rows + 2 * PAD, cols), bf16)
    hbm = pl.BlockSpec(memory_space=pl.ANY)
    smem = pl.BlockSpec(memory_space=pltpu.SMEM)
    result = pl.pallas_call(
        functools.partial(kernel, n),
        out_shape=jax.ShapeDtypeStruct((block, chunks, 128), f32),
        in_specs=[hbm] * 5 + [smem] * 3,
        out_specs=pl.BlockSpec(memory_space=pltpu.VMEM),
        scratch_shapes=[
            vm(wavefields.shape, f32),
            plane, plane, plane, plane,
            ext, ext,
            plane, plane, plane, plane, plane,
            vm((2 * rows, rows + 2 * PAD), bf16),
            vm((cols, cols), bf16),
            vm((cols, cols), bf16),
            table, table, table, table,
            vm((bins * group, rows), f32),
            vm((bins * group, rows), f32),
            vm((patches * chunks, 2 * angles), f32),
            vm((n * patches, chunks, 2 * angles), bf16),
            pltpu.SemaphoreType.DMA((6,)),
            pltpu.SemaphoreType.DMA((2, 2, pairs)),
            pltpu.SemaphoreType.DMA((2, 2, pairs)),
            pltpu.SemaphoreType.DMA((4 * high,)),
            pltpu.SemaphoreType.DMA((n,)),
        ],
        compiler_params=pltpu.CompilerParams(
            collective_id=0, has_side_effects=True, vmem_limit_bytes=48 * 1024 * 1024
        ),
        name="imaging",
    )(wavefields, courant, epsilon, anisotropy_delta, tilt_angle, loc_patch, slab_counts, angle_table)
    return result.reshape(block, chunks * 128)


def solution(mesh):
    return jax.shard_map(
        functools.partial(per_device, mesh.shape["slab"]),
        mesh=mesh,
        in_specs=(
            P(None, None, "groups", "slab", None),
            P("slab", None),
            P("slab", None),
            P("slab", None),
            P("slab", None),
            P(),
            P(),
            P(),
        ),
        out_specs=P(("groups", "slab"), None),
        check_vma=False,
    )
```

```python
import functools
import math

import jax
import jax.numpy as jnp
from jax import lax
from jax.experimental import pallas as pl
from jax.experimental.pallas import tpu as pltpu
from jax.sharding import PartitionSpec as P

MESH = pl.DeviceIdType.MESH
PAD = 16
REACH = 4
SECOND_TERMS = (-205.0 / 72.0, 8.0 / 5.0, -1.0 / 5.0, 8.0 / 315.0, -1.0 / 560.0)
FIRST_TERMS = (4.0 / 5.0, -1.0 / 5.0, 4.0 / 105.0, -1.0 / 280.0)


def sincos_turns(u):
    quarter = jnp.round(4.0 * u)
    theta = (u - 0.25 * quarter) * (2.0 * math.pi)
    sq = theta * theta
    sine = theta + theta * sq * (
        -1.0 / 6 + sq * (1.0 / 120 + sq * (-1.0 / 5040 + sq * (1.0 / 362880)))
    )
    cosine = 1.0 + sq * (-0.5 + sq * (1.0 / 24 + sq * (-1.0 / 720 + sq * (1.0 / 40320))))
    q = quarter.astype(jnp.int32)
    odd = (q & 1) == 1
    s = jnp.where(odd, cosine, sine)
    c = jnp.where(odd, sine, cosine)
    s = jnp.where((q & 2) == 2, -s, s)
    c = jnp.where(((q + 1) & 2) == 2, -c, c)
    return s, c


def band(distance, second):
    taps = SECOND_TERMS[1:] if second else FIRST_TERMS
    out = jnp.zeros(distance.shape, jnp.float32)
    for offset in range(1, REACH + 1):
        weight = taps[offset - 1] / taps[0]
        out = jnp.where(distance == offset, weight, out)
        out = jnp.where(distance == -offset, weight if second else -weight, out)
    return out


def iota(shape, dim):
    return lax.broadcasted_iota(jnp.int32, shape, dim)


def dot(a, b):
    return jnp.dot(a, b, preferred_element_type=jnp.float32)


def kernel(
    n,
    wav,
    courant,
    epsilon,
    delta,
    tilt,
    loc,
    counts,
    angle,
    out,
    state,
    c_in,
    e_in,
    d_in,
    t_in,
    ext1,
    ext2,
    ca,
    cb,
    cd,
    ce,
    cr,
    zmat,
    x2mat,
    x1mat,
    cos1,
    sin1,
    cos2,
    sin2,
    yre,
    yim,
    img,
    gath,
    in_sem,
    halo_send,
    halo_recv,
    ag_send,
    ag_recv,
):
    me = lax.axis_index("slab")
    _, _, shots, rows, cols = wav.shape
    patches = cols // rows
    bins = rows // 2
    angles = angle.shape[0]
    pairs = 2 * shots
    group = 2 * shots * patches
    half = group // 2
    block = out.shape[0]
    chunks = bins * angles // 128
    split = 8

    loads = []
    for j, (src, dst) in enumerate(
        (
            (wav.at[:, 0:2], state.at[:, 0:2]),
            (tilt, t_in),
            (epsilon, e_in),
            (delta, d_in),
            (courant, c_in),
            (wav.at[:, 2:4], state.at[:, 2:4]),
        )
    ):
        copy = pltpu.make_async_copy(src, dst, in_sem.at[j])
        copy.start()
        loads.append(copy)

    zero = jnp.zeros((2 * pairs, PAD, cols), jnp.bfloat16)
    for ext in (ext1, ext2):
        ext[:, 0:PAD, :] = zero
        ext[:, PAD + rows :, :] = zero

    barrier = pltpu.get_barrier_semaphore()
    for d in range(1, n):
        pl.semaphore_signal(
            barrier, inc=1, device_id={"slab": lax.rem(me + d, n)}, device_id_type=MESH
        )

    tall = rows + 2 * PAD
    reach = iota((rows, tall), 1) - PAD - iota((rows, tall), 0)
    zmat[0:rows] = band(reach, True).astype(jnp.bfloat16)
    zmat[rows:] = band(reach, False).astype(jnp.bfloat16)
    wide = iota((cols, cols), 0) - iota((cols, cols), 1)
    x2mat[...] = band(wide, True).astype(jnp.bfloat16)
    x1mat[...] = band(wide, False).astype(jnp.bfloat16)

    lanes = 2 * angles
    modulus = 16 * rows
    lane = iota((1, lanes), 1)
    slope = jnp.zeros((1, lanes), jnp.int32)
    for a in range(angles):
        slope = jnp.where(lane % angles == a, angle[a], slope)
    step = slope * iota((rows, lanes), 0)
    turn = jnp.where(iota((rows, lanes), 1) >= angles, modulus // 4, 0)
    scale = 1.0 / math.sqrt(rows)

    def phases(k, carry):
        j = jnp.bitwise_and(k * split * step, modulus - 1)
        s, c = sincos_turns(j.astype(jnp.float32) * (1.0 / modulus))
        cos1[k] = c
        sin1[k] = s
        j = jnp.bitwise_and(k * step + turn, modulus - 1)
        s, c = sincos_turns(j.astype(jnp.float32) * (1.0 / modulus))
        cos2[k] = c * scale
        sin2[k] = s * scale
        return carry

    lax.fori_loop(0, split, phases, 0)

    pl.semaphore_wait(barrier, n - 1)
    loads[0].wait()

    up = jnp.maximum(me - 1, 0)
    down = jnp.minimum(me + 1, n - 1)

    def halo(ext, step, i, upward):
        first = pl.ds(2 * i, 2)
        if upward:
            src = ext.at[first, PAD : 2 * PAD, :]
            dst = ext.at[first, PAD + rows : 2 * PAD + rows, :]
        else:
            src = ext.at[first, rows : PAD + rows, :]
            dst = ext.at[first, 0:PAD, :]
        way = 0 if upward else 1
        return pltpu.make_async_remote_copy(
            src_ref=src,
            dst_ref=dst,
            send_sem=halo_send.at[step, way, i],
            recv_sem=halo_recv.at[step, way, i],
            device_id={"slab": up if upward else down},
            device_id_type=MESH,
        )

    def send(ext, step, i):
        @pl.when(me > 0)
        def _():
            halo(ext, step, i, True).start()

        @pl.when(me < n - 1)
        def _():
            halo(ext, step, i, False).start()

    def receive(ext, step, i):
        @pl.when(me > 0)
        def _():
            halo(ext, step, i, False).wait_recv()

        @pl.when(me < n - 1)
        def _():
            halo(ext, step, i, True).wait_recv()

    def finish(ext, step, i):
        @pl.when(me > 0)
        def _():
            halo(ext, step, i, True).wait_send()

        @pl.when(me < n - 1)
        def _():
            halo(ext, step, i, False).wait_send()

    def convert(i, carry):
        f, s = i // shots, i % shots
        for w in range(2):
            ext1[2 * i + w, PAD : PAD + rows, :] = state[f, w, s].astype(jnp.bfloat16)
        send(ext1, 0, i)
        return carry

    lax.fori_loop(0, pairs, convert, 0)

    for copy in loads[1:5]:
        copy.wait()
    sine, cosine = sincos_turns(t_in[...] * (1.0 / math.pi))
    second_scale, first_scale = SECOND_TERMS[1], FIRST_TERMS[0]
    ca[...] = (0.5 * second_scale) * (1.0 - cosine)
    cb[...] = (0.5 * second_scale) * (1.0 + cosine)
    cd[...] = (first_scale * first_scale) * sine
    ce[...] = c_in[...] * (1.0 + 2.0 * e_in[...])
    cr[...] = c_in[...] * jnp.sqrt(1.0 + 2.0 * d_in[...])
    loads[5].wait()

    centre = SECOND_TERMS[0]

    def terms(ext, field):
        z = dot(zmat[...], ext[field])
        xx = dot(ext[field, PAD : PAD + rows, :], x2mat[...])
        xz = dot(z[rows:].astype(jnp.bfloat16), x1mat[...])
        return xx, z[:rows], xz

    def first(i, carry):
        f, s = i // shots, i % shots
        receive(ext1, 0, i)
        xx, zz, xz = terms(ext1, 2 * i)
        across = cb[...] * xx + ca[...] * zz - cd[...] * xz + centre * state[f, 0, s]
        xx, zz, xz = terms(ext1, 2 * i + 1)
        along = ca[...] * xx + cb[...] * zz + cd[...] * xz + centre * state[f, 1, s]
        p = 2.0 * state[f, 0, s] - state[f, 2, s] + ce[...] * across + cr[...] * along
        q = 2.0 * state[f, 1, s] - state[f, 3, s] + cr[...] * across + c_in[...] * along
        state[f, 2, s] = p
        state[f, 3, s] = q
        ext2[2 * i, PAD : PAD + rows, :] = p.astype(jnp.bfloat16)
        ext2[2 * i + 1, PAD : PAD + rows, :] = q.astype(jnp.bfloat16)
        send(ext2, 1, i)
        return carry

    lax.fori_loop(0, pairs, first, 0)

    kk = iota((rows, rows), 0)
    zz_ = iota((rows, rows), 1)
    turns = jnp.bitwise_and(jnp.where(kk >= bins, kk - bins, kk) * zz_, rows - 1)
    s_t, c_t = sincos_turns(turns.astype(jnp.float32) * (1.0 / rows))
    table = jnp.where(kk >= bins, -s_t, c_t) * scale
    table_hi = table.astype(jnp.bfloat16)
    table_lo = (table - table_hi.astype(jnp.float32)).astype(jnp.bfloat16)
    table = jnp.concatenate([table_hi, table_hi], axis=1)

    for i in range(pairs):
        f, s = i // shots, i % shots
        receive(ext2, 1, i)
        xx, zz, xz = terms(ext2, 2 * i)
        across = cb[...] * xx + ca[...] * zz - cd[...] * xz + centre * state[f, 2, s]
        xx, zz, xz = terms(ext2, 2 * i + 1)
        along = ca[...] * xx + cb[...] * zz + cd[...] * xz + centre * state[f, 3, s]
        p = 2.0 * state[f, 2, s] - state[f, 0, s] + ce[...] * across + cr[...] * along
        p_hi = p.astype(jnp.bfloat16)
        p_lo = (p - p_hi.astype(jnp.float32)).astype(jnp.bfloat16)
        spectrum = dot(table, jnp.concatenate([p_hi, p_lo], axis=0)) + dot(table_lo, p_hi)
        for m in range(patches):
            part = spectrum[:, m * rows : (m + 1) * rows]
            slot = i * patches + m
            yre[pl.ds(slot, bins, stride=group), :] = part[:bins]
            yim[pl.ds(slot, bins, stride=group), :] = part[bins:]

    def stack(k):
        k1, k2 = k // split, k % split
        c1, s1, c2, s2 = cos1[k1], sin1[k1], cos2[k2], sin2[k2]
        weights = jnp.concatenate([c1 * c2 - s1 * s2, s1 * c2 + c1 * s2], axis=0)
        at = pl.ds(pl.multiple_of(k * group, group), group)
        data = jnp.concatenate([yre[at, :], yim[at, :]], axis=1)
        st = dot(data.astype(jnp.bfloat16), weights.astype(jnp.bfloat16))
        prod = st[:half] * st[half:]
        total = prod[:patches]
        for shot in range(1, shots):
            total = total + prod[shot * patches : (shot + 1) * patches]
        return total + pltpu.roll(total, angles, 1)

    side = iota((patches, lanes), 1)

    def images(t, carry):
        both = jnp.where(side < angles, stack(2 * t), stack(2 * t + 1))
        img[pl.ds(t, patches, stride=chunks), :] = both
        return carry

    lax.fori_loop(0, chunks, images, 0)

    live = iota((patches, chunks, lanes), 0) < counts[me]
    own = jnp.where(live, img[...].reshape(patches, chunks, lanes), 0.0)
    gath[pl.ds(me * patches, patches)] = own.astype(jnp.bfloat16)

    high = n // 4
    h, m, l = me // 4, (me // 2) % 2, me % 2
    sent = []

    def ident(a, b, c):
        return a * 4 + b * 2 + c

    def pass_on(b, target):
        at = gath.at[pl.ds(b * patches, patches)]
        copy = pltpu.make_async_remote_copy(
            src_ref=at,
            dst_ref=at,
            send_sem=ag_send.at[len(sent)],
            recv_sem=ag_recv.at[b],
            device_id={"slab": target},
            device_id_type=MESH,
        )
        copy.start()
        sent.append(copy)

    def arrive(b):
        at = gath.at[pl.ds(b * patches, patches)]
        pltpu.make_async_remote_copy(
            src_ref=at,
            dst_ref=at,
            send_sem=ag_send.at[0],
            recv_sem=ag_recv.at[b],
            device_id={"slab": ident(h, m, 1 - l)},
            device_id_type=MESH,
        ).wait_recv()

    mid, low = ident(h, 1 - m, l), ident(h, m, 1 - l)
    for d in range(1, high):
        pass_on(me, ident(lax.rem(h + d, high), m, l))
    pass_on(me, mid)
    pass_on(me, low)
    for d in range(1, high):
        b = ident(lax.rem(h + high - d, high), m, l)
        arrive(b)
        pass_on(b, mid)
        pass_on(b, low)
    for d in range(high):
        b = ident(lax.rem(h + high - d, high), 1 - m, l)
        arrive(b)
        pass_on(b, low)
    for d in range(high):
        a = lax.rem(h + high - d, high)
        arrive(ident(a, m, 1 - l))
        arrive(ident(a, 1 - m, 1 - l))

    for g in range(block):
        out[g] = gath[loc[me * block + g]].astype(jnp.float32)

    for copy in sent:
        copy.wait_send()
    for i in range(pairs):
        finish(ext1, 0, i)
        finish(ext2, 1, i)


def per_device(
    n, wavefields, courant, epsilon, anisotropy_delta, tilt_angle, loc_patch, slab_counts, angle_table
):
    _, _, shots, rows, cols = wavefields.shape
    patches = cols // rows
    bins = rows // 2
    angles = angle_table.shape[0]
    block = loc_patch.shape[0] // n
    chunks = bins * angles // 128
    pairs = 2 * shots
    group = pairs * patches
    high = n // 4
    f32, bf16 = jnp.float32, jnp.bfloat16
    vm = pltpu.VMEM
    plane = vm((rows, cols), f32)
    table = vm((8, rows, 2 * angles), f32)
    ext = vm((2 * pairs, rows + 2 * PAD, cols), bf16)
    hbm = pl.BlockSpec(memory_space=pltpu.HBM)
    smem = pl.BlockSpec(memory_space=pltpu.SMEM)
    result = pl.pallas_call(
        functools.partial(kernel, n),
        out_shape=jax.ShapeDtypeStruct((block, chunks, 128), f32),
        in_specs=[hbm] * 5 + [smem] * 3,
        out_specs=pl.BlockSpec(memory_space=pltpu.VMEM),
        scratch_shapes=[
            vm(wavefields.shape, f32),
            plane, plane, plane, plane,
            ext, ext,
            plane, plane, plane, plane, plane,
            vm((2 * rows, rows + 2 * PAD), bf16),
            vm((cols, cols), bf16),
            vm((cols, cols), bf16),
            table, table, table, table,
            vm((bins * group, rows), f32),
            vm((bins * group, rows), f32),
            vm((patches * chunks, 2 * angles), f32),
            vm((n * patches, chunks, 2 * angles), bf16),
            pltpu.SemaphoreType.DMA((6,)),
            pltpu.SemaphoreType.DMA((2, 2, pairs)),
            pltpu.SemaphoreType.DMA((2, 2, pairs)),
            pltpu.SemaphoreType.DMA((4 * high,)),
            pltpu.SemaphoreType.DMA((n,)),
        ],
        compiler_params=pltpu.CompilerParams(
            collective_id=0, has_side_effects=True, vmem_limit_bytes=60 * 1024 * 1024
        ),
        name="imaging",
    )(wavefields, courant, epsilon, anisotropy_delta, tilt_angle, loc_patch, slab_counts, angle_table)
    return result.reshape(block, chunks * 128)


def solution(mesh):
    return jax.shard_map(
        functools.partial(per_device, mesh.shape["slab"]),
        mesh=mesh,
        in_specs=(
            P(None, None, "groups", "slab", None),
            P("slab", None),
            P("slab", None),
            P("slab", None),
            P("slab", None),
            P(),
            P(),
            P(),
        ),
        out_specs=P(("groups", "slab"), None),
        check_vma=False,
    )
```

```python
import functools
import math

import jax
import jax.numpy as jnp
from jax import lax
from jax.experimental import pallas as pl
from jax.experimental.pallas import tpu as pltpu
from jax.sharding import PartitionSpec as P

MESH = pl.DeviceIdType.MESH
PAD = 16
REACH = 4
LANES = 128
SECOND_TERMS = (-205.0 / 72.0, 8.0 / 5.0, -1.0 / 5.0, 8.0 / 315.0, -1.0 / 560.0)
FIRST_TERMS = (4.0 / 5.0, -1.0 / 5.0, 4.0 / 105.0, -1.0 / 280.0)


def sincos_turns(u):
    quarter = jnp.round(4.0 * u)
    theta = (u - 0.25 * quarter) * (2.0 * math.pi)
    sq = theta * theta
    sine = theta + theta * sq * (
        -1.0 / 6 + sq * (1.0 / 120 + sq * (-1.0 / 5040 + sq * (1.0 / 362880)))
    )
    cosine = 1.0 + sq * (-0.5 + sq * (1.0 / 24 + sq * (-1.0 / 720 + sq * (1.0 / 40320))))
    q = quarter.astype(jnp.int32)
    odd = (q & 1) == 1
    s = jnp.where(odd, cosine, sine)
    c = jnp.where(odd, sine, cosine)
    s = jnp.where((q & 2) == 2, -s, s)
    c = jnp.where(((q + 1) & 2) == 2, -c, c)
    return s, c


def band(distance, second):
    taps = SECOND_TERMS[1:] if second else FIRST_TERMS
    out = jnp.zeros(distance.shape, jnp.float32)
    for offset in range(1, REACH + 1):
        weight = taps[offset - 1] / taps[0]
        out = jnp.where(distance == offset, weight, out)
        out = jnp.where(distance == -offset, weight if second else -weight, out)
    return out


def iota(shape, dim):
    return lax.broadcasted_iota(jnp.int32, shape, dim)


def dot(a, b):
    return jnp.dot(a, b, preferred_element_type=jnp.float32)


def kernel(
    n,
    wav,
    courant,
    epsilon,
    delta,
    tilt,
    loc,
    counts,
    angle,
    out,
    state,
    c_in,
    e_in,
    d_in,
    t_in,
    ext1,
    ext2,
    ca,
    cb,
    cd,
    ce,
    cr,
    zmat,
    x2mat,
    x1mat,
    x2edge,
    x1edge,
    step_c,
    step_s,
    slant,
    cos1,
    sin1,
    cos2,
    sin2,
    yre,
    yim,
    img,
    gath,
    in_sem,
    halo_send,
    halo_recv,
    ag_send,
    ag_recv,
):
    me = lax.axis_index("slab")
    _, _, shots, rows, cols = wav.shape
    patches = cols // rows
    bins = rows // 2
    angles = angle.shape[0]
    pairs = 2 * shots
    group = 2 * shots * patches
    half = group // 2
    block = out.shape[0]
    chunks = bins * angles // 128
    split = 8

    def load(j, src, dst):
        copy = pltpu.make_async_copy(src, dst, in_sem.at[j])
        copy.start()
        return copy

    def fields(i, first):
        f, s = i // shots, i % shots
        at = (f, pl.ds(first, 2), s)
        return load(4 + 2 * i + first // 2, wav.at[at], state.at[at])

    now, before = [fields(0, 0)], []
    coefs = [
        load(j, src, dst)
        for j, (src, dst) in enumerate(
            ((tilt, t_in), (epsilon, e_in), (delta, d_in), (courant, c_in))
        )
    ]
    for i in range(1, pairs):
        now.append(fields(i, 0))
        before.append(fields(i - 1, 2))
    before.append(fields(pairs - 1, 2))

    zero = jnp.zeros((2 * pairs, PAD, cols), jnp.bfloat16)
    for ext in (ext1, ext2):
        ext[:, 0:PAD, :] = zero
        ext[:, PAD + rows :, :] = zero

    barrier = pltpu.get_barrier_semaphore()
    for d in range(1, n):
        pl.semaphore_signal(
            barrier, inc=1, device_id={"slab": lax.rem(me + d, n)}, device_id_type=MESH
        )

    tall = rows + 2 * PAD
    reach = iota((rows, tall), 1) - PAD - iota((rows, tall), 0)
    zmat[0:rows] = band(reach, True).astype(jnp.bfloat16)
    zmat[rows:] = band(reach, False).astype(jnp.bfloat16)
    apart = iota((LANES, LANES), 0) - iota((LANES, LANES), 1)
    for mat, edge, second in ((x2mat, x2edge, True), (x1mat, x1edge, False)):
        here = band(apart, second).astype(jnp.bfloat16)
        left = band(apart - LANES, second).astype(jnp.bfloat16)
        right = band(apart + LANES, second).astype(jnp.bfloat16)
        mat[0:LANES, 0:LANES] = here
        mat[LANES:, LANES:] = here
        mat[0:LANES, LANES:] = left
        mat[LANES:, 0:LANES] = right
        edge[0] = left
        edge[1] = right

    lanes = 2 * angles
    modulus = 16 * rows
    lane = iota((1, lanes), 1)
    slope = jnp.zeros((1, lanes), jnp.int32)
    for a in range(angles):
        slope = jnp.where(lane % angles == a, angle[a], slope)
    step = slope * iota((rows, lanes), 0)
    scale = 1.0 / math.sqrt(rows)

    def phase(j):
        j = jnp.bitwise_and(j, modulus - 1)
        return sincos_turns(j.astype(jnp.float32) * (1.0 / modulus))

    one = jnp.ones((rows, lanes), jnp.float32)
    sin1[0], cos1[0] = 0.0 * one, one
    fine_s, fine_c = phase(step)
    coarse_s, coarse_c = phase(split * step)
    first_half = iota((rows, lanes), 1) < angles
    sin2[0] = jnp.where(first_half, 0.0, scale)
    cos2[0] = jnp.where(first_half, scale, 0.0)
    sin1[1], cos1[1] = coarse_s, coarse_c
    sin2[1] = jnp.where(first_half, fine_s, fine_c) * scale
    cos2[1] = jnp.where(first_half, fine_c, -fine_s) * scale

    def phases(k, carry):
        c, s = cos1[k], sin1[k]
        cos1[k + 1] = c * cos1[1] - s * sin1[1]
        sin1[k + 1] = s * cos1[1] + c * sin1[1]
        c, s = cos2[k], sin2[k]
        fc, fs = step_c[...], step_s[...]
        cos2[k + 1] = c * fc - s * fs
        sin2[k + 1] = s * fc + c * fs
        return carry

    step_c[...] = fine_c
    step_s[...] = fine_s
    lax.fori_loop(1, split - 1, phases, 0)

    pl.semaphore_wait(barrier, n - 1)

    up = jnp.maximum(me - 1, 0)
    down = jnp.minimum(me + 1, n - 1)

    def halo(ext, step, i, upward):
        first = pl.ds(2 * i, 2)
        if upward:
            src = ext.at[first, PAD : 2 * PAD, :]
            dst = ext.at[first, PAD + rows : 2 * PAD + rows, :]
        else:
            src = ext.at[first, rows : PAD + rows, :]
            dst = ext.at[first, 0:PAD, :]
        way = 0 if upward else 1
        return pltpu.make_async_remote_copy(
            src_ref=src,
            dst_ref=dst,
            send_sem=halo_send.at[step, way, i],
            recv_sem=halo_recv.at[step, way, i],
            device_id={"slab": up if upward else down},
            device_id_type=MESH,
        )

    def send(ext, step, i):
        @pl.when(me > 0)
        def _():
            halo(ext, step, i, True).start()

        @pl.when(me < n - 1)
        def _():
            halo(ext, step, i, False).start()

    def receive(ext, step, i):
        @pl.when(me > 0)
        def _():
            halo(ext, step, i, False).wait_recv()

        @pl.when(me < n - 1)
        def _():
            halo(ext, step, i, True).wait_recv()

    def finish(ext, step, i):
        @pl.when(me > 0)
        def _():
            halo(ext, step, i, True).wait_send()

        @pl.when(me < n - 1)
        def _():
            halo(ext, step, i, False).wait_send()

    def convert(i):
        f, s = i // shots, i % shots
        now[i].wait()
        for w in range(2):
            ext1[2 * i + w, PAD : PAD + rows, :] = state[f, w, s].astype(jnp.bfloat16)
        send(ext1, 0, i)

    convert(0)

    for copy in coefs:
        copy.wait()
    sine, cosine = sincos_turns(t_in[...] * (1.0 / math.pi))
    second_scale, first_scale = SECOND_TERMS[1], FIRST_TERMS[0]
    ca[...] = (0.5 * second_scale) * (1.0 - cosine)
    cb[...] = (0.5 * second_scale) * (1.0 + cosine)
    cd[...] = (first_scale * first_scale) * sine
    ce[...] = c_in[...] * (1.0 + 2.0 * e_in[...])
    cr[...] = c_in[...] * jnp.sqrt(1.0 + 2.0 * d_in[...])

    def slants(k1, carry):
        for k2 in range(split):
            k = k1 * split + k2
            for r in range(0, rows, 32):
                at = pl.ds(r, 32)
                c1, s1 = cos1[k1, at], sin1[k1, at]
                c2, s2 = cos2[k2, at], sin2[k2, at]
                slant[k, at, :] = (c1 * c2 - s1 * s2).astype(jnp.bfloat16)
                slant[k, pl.ds(rows + r, 32), :] = (s1 * c2 + c1 * s2).astype(jnp.bfloat16)
        return carry

    lax.fori_loop(0, bins // split, slants, 0)

    centre = SECOND_TERMS[0]

    wide = 2 * LANES

    def along_x(x, mat, edge):
        pieces = []
        for c in range(0, cols, wide):
            y = dot(x[:, c : c + wide], mat[...])
            low, top = y[:, :LANES], y[:, LANES:]
            if c > 0:
                low = low + dot(x[:, c - LANES : c], edge[0])
            if c + wide < cols:
                top = top + dot(x[:, c + wide : c + wide + LANES], edge[1])
            pieces += [low, top]
        return jnp.concatenate(pieces, axis=1)

    def terms(ext, i, p, q):
        zp = dot(zmat[...], ext[2 * i])
        zq = dot(zmat[...], ext[2 * i + 1])
        both = ext[2 * i : 2 * i + 2, PAD : PAD + rows, :].reshape(2 * rows, cols)
        xx = along_x(both, x2mat, x2edge)
        mixed = jnp.concatenate([zp[rows:], zq[rows:]], axis=0).astype(jnp.bfloat16)
        xz = along_x(mixed, x1mat, x1edge)
        a, b, d = ca[...], cb[...], cd[...]
        across = b * xx[:rows] + a * zp[:rows] - d * xz[:rows] + centre * p
        along = a * xx[rows:] + b * zq[:rows] + d * xz[rows:] + centre * q
        return across, along

    for i in range(pairs):
        f, s = i // shots, i % shots
        if i + 1 < pairs:
            convert(i + 1)
        before[i].wait()
        receive(ext1, 0, i)
        p0, q0 = state[f, 0, s], state[f, 1, s]
        across, along = terms(ext1, i, p0, q0)
        p = 2.0 * p0 - state[f, 2, s] + ce[...] * across + cr[...] * along
        q = 2.0 * q0 - state[f, 3, s] + cr[...] * across + c_in[...] * along
        state[f, 2, s] = p
        state[f, 3, s] = q
        ext2[2 * i, PAD : PAD + rows, :] = p.astype(jnp.bfloat16)
        ext2[2 * i + 1, PAD : PAD + rows, :] = q.astype(jnp.bfloat16)
        send(ext2, 1, i)

    kk = iota((rows, rows), 0)
    zz_ = iota((rows, rows), 1)
    turns = jnp.bitwise_and(jnp.where(kk >= bins, kk - bins, kk) * zz_, rows - 1)
    s_t, c_t = sincos_turns(turns.astype(jnp.float32) * (1.0 / rows))
    table = jnp.where(kk >= bins, -s_t, c_t) * scale
    table_hi = table.astype(jnp.bfloat16)
    table_lo = (table - table_hi.astype(jnp.float32)).astype(jnp.bfloat16)
    table = jnp.concatenate([table_hi, table_hi], axis=1)

    for i in range(pairs):
        f, s = i // shots, i % shots
        receive(ext2, 1, i)
        p1 = state[f, 2, s]
        across, along = terms(ext2, i, p1, state[f, 3, s])
        p = 2.0 * p1 - state[f, 0, s] + ce[...] * across + cr[...] * along
        p_hi = p.astype(jnp.bfloat16)
        p_lo = (p - p_hi.astype(jnp.float32)).astype(jnp.bfloat16)
        spectrum = dot(table, jnp.concatenate([p_hi, p_lo], axis=0)) + dot(table_lo, p_hi)
        for m in range(patches):
            part = spectrum[:, m * rows : (m + 1) * rows]
            slot = i * patches + m
            yre[pl.ds(slot, bins, stride=group), :] = part[:bins]
            yim[pl.ds(slot, bins, stride=group), :] = part[bins:]

    def stack(k):
        at = pl.ds(pl.multiple_of(k * group, group), group)
        data = jnp.concatenate([yre[at, :], yim[at, :]], axis=1)
        st = dot(data.astype(jnp.bfloat16), slant[k])
        prod = st[:half] * st[half:]
        total = prod[:patches]
        for shot in range(1, shots):
            total = total + prod[shot * patches : (shot + 1) * patches]
        return total

    side = iota((patches, lanes), 1) < angles
    unroll = 4

    def images(j, carry):
        for v in range(unroll):
            t = j * unroll + v
            even, odd = stack(2 * t), stack(2 * t + 1)
            keep = jnp.where(side, even, odd)
            give = jnp.where(side, odd, even)
            img[pl.ds(t, patches, stride=chunks), :] = keep + pltpu.roll(give, angles, 1)
        return carry

    live = iota((patches, chunks // 2, lanes), 0) < counts[me]

    def finish_half(w):
        per = chunks // (2 * unroll)
        lax.fori_loop(w * per, (w + 1) * per, images, 0)
        own = jnp.where(live, img[...].reshape(patches, chunks, lanes)[:, w * (chunks // 2) : (w + 1) * (chunks // 2)], 0.0)
        gath[pl.ds(me * patches, patches), w] = own.astype(jnp.bfloat16)

    high = n // 4
    h, m, l = me // 4, (me // 2) % 2, me % 2
    sent = []

    def ident(a, b, c):
        return a * 4 + b * 2 + c

    def pass_on(b, w, target):
        at = gath.at[pl.ds(b * patches, patches), w]
        copy = pltpu.make_async_remote_copy(
            src_ref=at,
            dst_ref=at,
            send_sem=ag_send.at[len(sent)],
            recv_sem=ag_recv.at[w, b],
            device_id={"slab": target},
            device_id_type=MESH,
        )
        copy.start()
        sent.append(copy)

    mid, low = ident(h, 1 - m, l), ident(h, m, 1 - l)

    def arrive(b, w):
        at = gath.at[pl.ds(b * patches, patches), w]
        pltpu.make_async_remote_copy(
            src_ref=at,
            dst_ref=at,
            send_sem=ag_send.at[0],
            recv_sem=ag_recv.at[w, b],
            device_id={"slab": low},
            device_id_type=MESH,
        ).wait_recv()

    for w in range(2):
        finish_half(w)
        pass_on(me, w, mid)
        for d in range(1, high):
            pass_on(me, w, ident(lax.rem(h + d, high), m, l))
        pass_on(me, w, low)
    for w in range(2):
        b = ident(h, 1 - m, l)
        arrive(b, w)
        pass_on(b, w, low)
        for d in range(1, high):
            a = lax.rem(h + high - d, high)
            b = ident(a, m, l)
            arrive(b, w)
            pass_on(b, w, mid)
            pass_on(b, w, low)
    for w in range(2):
        for d in range(1, high):
            b = ident(lax.rem(h + high - d, high), 1 - m, l)
            arrive(b, w)
            pass_on(b, w, low)
    for w in range(2):
        for d in range(high):
            a = lax.rem(h + high - d, high)
            arrive(ident(a, m, 1 - l), w)
            arrive(ident(a, 1 - m, 1 - l), w)

    for g in range(block):
        out[g] = gath[loc[me * block + g]].astype(jnp.float32).reshape(chunks, lanes)

    for copy in sent:
        copy.wait_send()
    for i in range(pairs):
        finish(ext1, 0, i)
        finish(ext2, 1, i)


def per_device(
    n, wavefields, courant, epsilon, anisotropy_delta, tilt_angle, loc_patch, slab_counts, angle_table
):
    _, _, shots, rows, cols = wavefields.shape
    patches = cols // rows
    bins = rows // 2
    angles = angle_table.shape[0]
    block = loc_patch.shape[0] // n
    chunks = bins * angles // 128
    pairs = 2 * shots
    group = pairs * patches
    high = n // 4
    f32, bf16 = jnp.float32, jnp.bfloat16
    vm = pltpu.VMEM
    plane = vm((rows, cols), f32)
    table = vm((8, rows, 2 * angles), f32)
    ext = vm((2 * pairs, rows + 2 * PAD, cols), bf16)
    hbm = pl.BlockSpec(memory_space=pltpu.HBM)
    smem = pl.BlockSpec(memory_space=pltpu.SMEM)
    result = pl.pallas_call(
        functools.partial(kernel, n),
        out_shape=jax.ShapeDtypeStruct((block, chunks, 128), f32),
        in_specs=[hbm] * 5 + [smem] * 3,
        out_specs=pl.BlockSpec(memory_space=pltpu.VMEM),
        scratch_shapes=[
            vm(wavefields.shape, f32),
            plane, plane, plane, plane,
            ext, ext,
            plane, plane, plane, plane, plane,
            vm((2 * rows, rows + 2 * PAD), bf16),
            vm((2 * LANES, 2 * LANES), bf16),
            vm((2 * LANES, 2 * LANES), bf16),
            vm((2, LANES, LANES), bf16),
            vm((2, LANES, LANES), bf16),
            vm((rows, 2 * angles), f32),
            vm((rows, 2 * angles), f32),
            vm((bins, 2 * rows, 2 * angles), bf16),
            table, table, table, table,
            vm((bins * group, rows), f32),
            vm((bins * group, rows), f32),
            vm((patches * chunks, 2 * angles), f32),
            vm((n * patches, 2, chunks // 2, 2 * angles), bf16),
            pltpu.SemaphoreType.DMA((4 + 2 * pairs,)),
            pltpu.SemaphoreType.DMA((2, 2, pairs)),
            pltpu.SemaphoreType.DMA((2, 2, pairs)),
            pltpu.SemaphoreType.DMA((8 * high,)),
            pltpu.SemaphoreType.DMA((2, n)),
        ],
        compiler_params=pltpu.CompilerParams(
            collective_id=0, has_side_effects=True, vmem_limit_bytes=60 * 1024 * 1024
        ),
        name="imaging",
    )(wavefields, courant, epsilon, anisotropy_delta, tilt_angle, loc_patch, slab_counts, angle_table)
    return result.reshape(block, chunks * 128)


def solution(mesh):
    return jax.shard_map(
        functools.partial(per_device, mesh.shape["slab"]),
        mesh=mesh,
        in_specs=(
            P(None, None, "groups", "slab", None),
            P("slab", None),
            P("slab", None),
            P("slab", None),
            P("slab", None),
            P(),
            P(),
            P(),
        ),
        out_specs=P(("groups", "slab"), None),
        check_vma=False,
    )
```

```python
import functools
import math

import jax
import jax.numpy as jnp
from jax import lax
from jax.experimental import pallas as pl
from jax.experimental.pallas import tpu as pltpu
from jax.sharding import PartitionSpec as P

MESH = pl.DeviceIdType.MESH
PAD = 16
REACH = 4
LANES = 128
SECOND_TERMS = (-205.0 / 72.0, 8.0 / 5.0, -1.0 / 5.0, 8.0 / 315.0, -1.0 / 560.0)
FIRST_TERMS = (4.0 / 5.0, -1.0 / 5.0, 4.0 / 105.0, -1.0 / 280.0)


def sincos_turns(u):
    quarter = jnp.round(4.0 * u)
    theta = (u - 0.25 * quarter) * (2.0 * math.pi)
    sq = theta * theta
    sine = theta + theta * sq * (
        -1.0 / 6 + sq * (1.0 / 120 + sq * (-1.0 / 5040 + sq * (1.0 / 362880)))
    )
    cosine = 1.0 + sq * (-0.5 + sq * (1.0 / 24 + sq * (-1.0 / 720 + sq * (1.0 / 40320))))
    q = quarter.astype(jnp.int32)
    odd = (q & 1) == 1
    s = jnp.where(odd, cosine, sine)
    c = jnp.where(odd, sine, cosine)
    s = jnp.where((q & 2) == 2, -s, s)
    c = jnp.where(((q + 1) & 2) == 2, -c, c)
    return s, c


def band(distance, second):
    taps = SECOND_TERMS[1:] if second else FIRST_TERMS
    out = jnp.zeros(distance.shape, jnp.float32)
    for offset in range(1, REACH + 1):
        weight = taps[offset - 1] / taps[0]
        out = jnp.where(distance == offset, weight, out)
        out = jnp.where(distance == -offset, weight if second else -weight, out)
    return out


def iota(shape, dim):
    return lax.broadcasted_iota(jnp.int32, shape, dim)


def dot(a, b):
    return jnp.dot(a, b, preferred_element_type=jnp.float32)


def kernel(
    n,
    wav,
    courant,
    epsilon,
    delta,
    tilt,
    loc,
    counts,
    angle,
    out,
    state,
    c_in,
    e_in,
    d_in,
    t_in,
    ext1,
    ext2,
    edges,
    halos,
    ca,
    cb,
    cd,
    ce,
    cr,
    zmat,
    x2mat,
    x1mat,
    x2edge,
    x1edge,
    step_c,
    step_s,
    slant,
    cos1,
    sin1,
    cos2,
    sin2,
    yre,
    yim,
    img,
    gath,
    in_sem,
    halo_send,
    halo_recv,
    ag_send,
    ag_recv,
):
    me = lax.axis_index("slab")
    _, _, shots, rows, cols = wav.shape
    patches = cols // rows
    bins = rows // 2
    angles = angle.shape[0]
    pairs = 2 * shots
    group = 2 * shots * patches
    half = group // 2
    block = out.shape[0]
    chunks = bins * angles // 128
    split = 8

    def load(j, src, dst):
        copy = pltpu.make_async_copy(src, dst, in_sem.at[j])
        copy.start()
        return copy

    def fields(i, first):
        f, s = i // shots, i % shots
        at = (f, pl.ds(first, 2), s)
        return load(4 + 2 * i + first // 2, wav.at[at], state.at[at])

    now = [fields(i, 0) for i in range(pairs)]
    coefs = [
        load(j, src, dst)
        for j, (src, dst) in enumerate(
            ((tilt, t_in), (epsilon, e_in), (delta, d_in), (courant, c_in))
        )
    ]
    before = [fields(i, 2) for i in range(pairs)]

    halos[...] = jnp.zeros(halos.shape, jnp.bfloat16)

    barrier = pltpu.get_barrier_semaphore()
    for d in range(1, n):
        pl.semaphore_signal(
            barrier, inc=1, device_id={"slab": lax.rem(me + d, n)}, device_id_type=MESH
        )

    tall = rows + 2 * PAD
    col = iota((rows, tall), 1)
    for w in range(2):
        source = jnp.where(col < PAD, col - 8 * w - 8, col - PAD)
        source = jnp.where(col >= PAD + rows, source - 8 * w, source)
        strange = (col < PAD) & (col // 8 != w)
        strange |= (col >= PAD + rows) & ((col - PAD - rows) // 8 != w)
        reach = jnp.where(strange, rows, source - iota((rows, tall), 0))
        zmat[w, 0:rows] = band(reach, True).astype(jnp.bfloat16)
        zmat[w, rows:] = band(reach, False).astype(jnp.bfloat16)
    apart = iota((LANES, LANES), 0) - iota((LANES, LANES), 1)
    for mat, edge, second in ((x2mat, x2edge, True), (x1mat, x1edge, False)):
        here = band(apart, second).astype(jnp.bfloat16)
        left = band(apart - LANES, second).astype(jnp.bfloat16)
        right = band(apart + LANES, second).astype(jnp.bfloat16)
        mat[0:LANES, 0:LANES] = here
        mat[LANES:, LANES:] = here
        mat[0:LANES, LANES:] = left
        mat[LANES:, 0:LANES] = right
        edge[0] = left
        edge[1] = right

    lanes = 2 * angles
    modulus = 16 * rows
    lane = iota((1, lanes), 1)
    slope = jnp.zeros((1, lanes), jnp.int32)
    for a in range(angles):
        slope = jnp.where(lane % angles == a, angle[a], slope)
    step = slope * iota((rows, lanes), 0)
    scale = 1.0 / math.sqrt(rows)

    def phase(j):
        j = jnp.bitwise_and(j, modulus - 1)
        return sincos_turns(j.astype(jnp.float32) * (1.0 / modulus))

    one = jnp.ones((rows, lanes), jnp.float32)
    sin1[0], cos1[0] = 0.0 * one, one
    fine_s, fine_c = phase(step)
    coarse_s, coarse_c = phase(split * step)
    first_half = iota((rows, lanes), 1) < angles
    sin2[0] = jnp.where(first_half, 0.0, scale)
    cos2[0] = jnp.where(first_half, scale, 0.0)
    sin1[1], cos1[1] = coarse_s, coarse_c
    sin2[1] = jnp.where(first_half, fine_s, fine_c) * scale
    cos2[1] = jnp.where(first_half, fine_c, -fine_s) * scale

    def phases(k, carry):
        c, s = cos1[k], sin1[k]
        cos1[k + 1] = c * cos1[1] - s * sin1[1]
        sin1[k + 1] = s * cos1[1] + c * sin1[1]
        c, s = cos2[k], sin2[k]
        fc, fs = step_c[...], step_s[...]
        cos2[k + 1] = c * fc - s * fs
        sin2[k + 1] = s * fc + c * fs
        return carry

    step_c[...] = fine_c
    step_s[...] = fine_s
    lax.fori_loop(1, split - 1, phases, 0)

    pl.semaphore_wait(barrier, n - 1)

    up = jnp.maximum(me - 1, 0)
    down = jnp.minimum(me + 1, n - 1)

    def halo(step, i, upward):
        way = 0 if upward else 1
        return pltpu.make_async_remote_copy(
            src_ref=edges.at[step, i, way],
            dst_ref=halos.at[step, i, way],
            send_sem=halo_send.at[step, way, i],
            recv_sem=halo_recv.at[step, way, i],
            device_id={"slab": up if upward else down},
            device_id_type=MESH,
        )

    def put_edges(step, i, p, q):
        for way, cut in ((0, slice(0, 8)), (1, slice(rows - 8, rows))):
            both = jnp.concatenate([p[cut], q[cut]], axis=0)
            edges[step, i, way] = both.astype(jnp.bfloat16)

    def send(step, i):
        @pl.when(me > 0)
        def _():
            halo(step, i, True).start()

        @pl.when(me < n - 1)
        def _():
            halo(step, i, False).start()

    def receive(step, i):
        @pl.when(me > 0)
        def _():
            halo(step, i, False).wait_recv()

        @pl.when(me < n - 1)
        def _():
            halo(step, i, True).wait_recv()

    def finish(step, i):
        @pl.when(me > 0)
        def _():
            halo(step, i, True).wait_send()

        @pl.when(me < n - 1)
        def _():
            halo(step, i, False).wait_send()

    def convert(i):
        f, s = i // shots, i % shots
        for w in range(2):
            ext1[2 * i + w] = state[f, w, s].astype(jnp.bfloat16)

    for i in range(pairs):
        f, s = i // shots, i % shots
        now[i].wait()
        put_edges(0, i, state[f, 0, s], state[f, 1, s])
        send(0, i)
    for i in range(pairs):
        convert(i)

    for copy in coefs:
        copy.wait()
    sine, cosine = sincos_turns(t_in[...] * (1.0 / math.pi))
    second_scale, first_scale = SECOND_TERMS[1], FIRST_TERMS[0]
    ca[...] = (0.5 * second_scale) * (1.0 - cosine)
    cb[...] = (0.5 * second_scale) * (1.0 + cosine)
    cd[...] = (first_scale * first_scale) * sine
    ce[...] = c_in[...] * (1.0 + 2.0 * e_in[...])
    cr[...] = c_in[...] * jnp.sqrt(1.0 + 2.0 * d_in[...])

    def slants(k1, carry):
        for k2 in range(split):
            k = k1 * split + k2
            for r in range(0, rows, 32):
                at = pl.ds(r, 32)
                c1, s1 = cos1[k1, at], sin1[k1, at]
                c2, s2 = cos2[k2, at], sin2[k2, at]
                slant[k, at, :] = (c1 * c2 - s1 * s2).astype(jnp.bfloat16)
                slant[k, pl.ds(rows + r, 32), :] = (s1 * c2 + c1 * s2).astype(jnp.bfloat16)
        return carry

    lax.fori_loop(0, bins // split, slants, 0)

    centre = SECOND_TERMS[0]

    wide = 2 * LANES

    def along_x(x, mat, edge):
        pieces = []
        for c in range(0, cols, wide):
            y = dot(x[:, c : c + wide], mat[...])
            low, top = y[:, :LANES], y[:, LANES:]
            if c > 0:
                low = low + dot(x[:, c - LANES : c], edge[0])
            if c + wide < cols:
                top = top + dot(x[:, c + wide : c + wide + LANES], edge[1])
            pieces += [low, top]
        return jnp.concatenate(pieces, axis=1)

    def terms(ext, step, i, p, q):
        above, below = halos[step, i, 1], halos[step, i, 0]
        zp = dot(zmat[0], jnp.concatenate([above, ext[2 * i], below], axis=0))
        zq = dot(zmat[1], jnp.concatenate([above, ext[2 * i + 1], below], axis=0))
        both = ext[2 * i : 2 * i + 2].reshape(2 * rows, cols)
        xx = along_x(both, x2mat, x2edge)
        mixed = jnp.concatenate([zp[rows:], zq[rows:]], axis=0).astype(jnp.bfloat16)
        xz = along_x(mixed, x1mat, x1edge)
        a, b, d = ca[...], cb[...], cd[...]
        across = b * xx[:rows] + a * zp[:rows] - d * xz[:rows] + centre * p
        along = a * xx[rows:] + b * zq[:rows] + d * xz[rows:] + centre * q
        return across, along

    for i in range(pairs):
        f, s = i // shots, i % shots
        before[i].wait()
        receive(0, i)
        p0, q0 = state[f, 0, s], state[f, 1, s]
        across, along = terms(ext1, 0, i, p0, q0)
        p = 2.0 * p0 - state[f, 2, s] + ce[...] * across + cr[...] * along
        q = 2.0 * q0 - state[f, 3, s] + cr[...] * across + c_in[...] * along
        state[f, 2, s] = p
        state[f, 3, s] = q
        put_edges(1, i, p, q)
        ext2[2 * i] = p.astype(jnp.bfloat16)
        ext2[2 * i + 1] = q.astype(jnp.bfloat16)
        send(1, i)

    kk = iota((rows, rows), 0)
    zz_ = iota((rows, rows), 1)
    turns = jnp.bitwise_and(jnp.where(kk >= bins, kk - bins, kk) * zz_, rows - 1)
    s_t, c_t = sincos_turns(turns.astype(jnp.float32) * (1.0 / rows))
    table = jnp.where(kk >= bins, -s_t, c_t) * scale
    table_hi = table.astype(jnp.bfloat16)
    table_lo = (table - table_hi.astype(jnp.float32)).astype(jnp.bfloat16)
    table = jnp.concatenate([table_hi, table_hi], axis=1)

    for i in range(pairs):
        f, s = i // shots, i % shots
        receive(1, i)
        p1 = state[f, 2, s]
        across, along = terms(ext2, 1, i, p1, state[f, 3, s])
        p = 2.0 * p1 - state[f, 0, s] + ce[...] * across + cr[...] * along
        p_hi = p.astype(jnp.bfloat16)
        p_lo = (p - p_hi.astype(jnp.float32)).astype(jnp.bfloat16)
        spectrum = dot(table, jnp.concatenate([p_hi, p_lo], axis=0)) + dot(table_lo, p_hi)
        for m in range(patches):
            part = spectrum[:, m * rows : (m + 1) * rows]
            slot = i * patches + m
            yre[pl.ds(slot, bins, stride=group), :] = part[:bins]
            yim[pl.ds(slot, bins, stride=group), :] = part[bins:]

    def stack(k):
        at = pl.ds(pl.multiple_of(k * group, group), group)
        data = jnp.concatenate([yre[at, :], yim[at, :]], axis=1)
        st = dot(data.astype(jnp.bfloat16), slant[k])
        prod = st[:half] * st[half:]
        total = prod[:patches]
        for shot in range(1, shots):
            total = total + prod[shot * patches : (shot + 1) * patches]
        return total

    side = iota((patches, lanes), 1) < angles
    unroll = 4

    def images(j, carry):
        for v in range(unroll):
            t = j * unroll + v
            even, odd = stack(2 * t), stack(2 * t + 1)
            keep = jnp.where(side, even, odd)
            give = jnp.where(side, odd, even)
            img[pl.ds(t, patches, stride=chunks), :] = keep + pltpu.roll(give, angles, 1)
        return carry

    live = iota((patches, chunks // 2, lanes), 0) < counts[me]

    def finish_half(w):
        per = chunks // (2 * unroll)
        lax.fori_loop(w * per, (w + 1) * per, images, 0)
        own = jnp.where(live, img[...].reshape(patches, chunks, lanes)[:, w * (chunks // 2) : (w + 1) * (chunks // 2)], 0.0)
        gath[pl.ds(me * patches, patches), w] = own.astype(jnp.bfloat16)

    high = n // 4
    h, m, l = me // 4, (me // 2) % 2, me % 2
    sent = []

    def ident(a, b, c):
        return a * 4 + b * 2 + c

    def pass_on(b, w, target):
        at = gath.at[pl.ds(b * patches, patches), w]
        copy = pltpu.make_async_remote_copy(
            src_ref=at,
            dst_ref=at,
            send_sem=ag_send.at[len(sent)],
            recv_sem=ag_recv.at[w, b],
            device_id={"slab": target},
            device_id_type=MESH,
        )
        copy.start()
        sent.append(copy)

    mid, low = ident(h, 1 - m, l), ident(h, m, 1 - l)

    def arrive(b, w):
        at = gath.at[pl.ds(b * patches, patches), w]
        pltpu.make_async_remote_copy(
            src_ref=at,
            dst_ref=at,
            send_sem=ag_send.at[0],
            recv_sem=ag_recv.at[w, b],
            device_id={"slab": low},
            device_id_type=MESH,
        ).wait_recv()

    for w in range(2):
        finish_half(w)
        pass_on(me, w, mid)
        for d in range(1, high):
            pass_on(me, w, ident(lax.rem(h + d, high), m, l))
        pass_on(me, w, low)
    for w in range(2):
        b = ident(h, 1 - m, l)
        arrive(b, w)
        pass_on(b, w, low)
        for d in range(1, high):
            a = lax.rem(h + high - d, high)
            b = ident(a, m, l)
            arrive(b, w)
            pass_on(b, w, mid)
            pass_on(b, w, low)
    for w in range(2):
        for d in range(1, high):
            b = ident(lax.rem(h + high - d, high), 1 - m, l)
            arrive(b, w)
            pass_on(b, w, low)
    for w in range(2):
        for d in range(high):
            a = lax.rem(h + high - d, high)
            arrive(ident(a, m, 1 - l), w)
            arrive(ident(a, 1 - m, 1 - l), w)

    for g in range(block):
        out[g] = gath[loc[me * block + g]].astype(jnp.float32).reshape(chunks, lanes)

    for copy in sent:
        copy.wait_send()
    for i in range(pairs):
        finish(0, i)
        finish(1, i)


def per_device(
    n, wavefields, courant, epsilon, anisotropy_delta, tilt_angle, loc_patch, slab_counts, angle_table
):
    _, _, shots, rows, cols = wavefields.shape
    patches = cols // rows
    bins = rows // 2
    angles = angle_table.shape[0]
    block = loc_patch.shape[0] // n
    chunks = bins * angles // 128
    pairs = 2 * shots
    group = pairs * patches
    high = n // 4
    f32, bf16 = jnp.float32, jnp.bfloat16
    vm = pltpu.VMEM
    plane = vm((rows, cols), f32)
    table = vm((8, rows, 2 * angles), f32)
    ext = vm((2 * pairs, rows, cols), bf16)
    rims = vm((2, pairs, 2, PAD, cols), bf16)
    hbm = pl.BlockSpec(memory_space=pltpu.HBM)
    smem = pl.BlockSpec(memory_space=pltpu.SMEM)
    result = pl.pallas_call(
        functools.partial(kernel, n),
        out_shape=jax.ShapeDtypeStruct((block, chunks, 128), f32),
        in_specs=[hbm] * 5 + [smem] * 3,
        out_specs=pl.BlockSpec(memory_space=pltpu.VMEM),
        scratch_shapes=[
            vm(wavefields.shape, f32),
            plane, plane, plane, plane,
            ext, ext, rims, rims,
            plane, plane, plane, plane, plane,
            vm((2, 2 * rows, rows + 2 * PAD), bf16),
            vm((2 * LANES, 2 * LANES), bf16),
            vm((2 * LANES, 2 * LANES), bf16),
            vm((2, LANES, LANES), bf16),
            vm((2, LANES, LANES), bf16),
            vm((rows, 2 * angles), f32),
            vm((rows, 2 * angles), f32),
            vm((bins, 2 * rows, 2 * angles), bf16),
            table, table, table, table,
            vm((bins * group, rows), f32),
            vm((bins * group, rows), f32),
            vm((patches * chunks, 2 * angles), f32),
            vm((n * patches, 2, chunks // 2, 2 * angles), bf16),
            pltpu.SemaphoreType.DMA((4 + 2 * pairs,)),
            pltpu.SemaphoreType.DMA((2, 2, pairs)),
            pltpu.SemaphoreType.DMA((2, 2, pairs)),
            pltpu.SemaphoreType.DMA((8 * high,)),
            pltpu.SemaphoreType.DMA((2, n)),
        ],
        compiler_params=pltpu.CompilerParams(
            collective_id=0, has_side_effects=True, vmem_limit_bytes=60 * 1024 * 1024
        ),
        name="imaging",
    )(wavefields, courant, epsilon, anisotropy_delta, tilt_angle, loc_patch, slab_counts, angle_table)
    return result.reshape(block, chunks * 128)


def solution(mesh):
    return jax.shard_map(
        functools.partial(per_device, mesh.shape["slab"]),
        mesh=mesh,
        in_specs=(
            P(None, None, "groups", "slab", None),
            P("slab", None),
            P("slab", None),
            P("slab", None),
            P("slab", None),
            P(),
            P(),
            P(),
        ),
        out_specs=P(("groups", "slab"), None),
        check_vma=False,
    )
```

```python
import functools
import math

import jax
import jax.numpy as jnp
from jax import lax
from jax.experimental import pallas as pl
from jax.experimental.pallas import tpu as pltpu
from jax.sharding import PartitionSpec as P

MESH = pl.DeviceIdType.MESH
PAD = 16
REACH = 4
LANES = 128
SECOND_TERMS = (-205.0 / 72.0, 8.0 / 5.0, -1.0 / 5.0, 8.0 / 315.0, -1.0 / 560.0)
FIRST_TERMS = (4.0 / 5.0, -1.0 / 5.0, 4.0 / 105.0, -1.0 / 280.0)


def sincos_turns(u):
    quarter = jnp.round(4.0 * u)
    theta = (u - 0.25 * quarter) * (2.0 * math.pi)
    sq = theta * theta
    sine = theta + theta * sq * (
        -1.0 / 6 + sq * (1.0 / 120 + sq * (-1.0 / 5040 + sq * (1.0 / 362880)))
    )
    cosine = 1.0 + sq * (-0.5 + sq * (1.0 / 24 + sq * (-1.0 / 720 + sq * (1.0 / 40320))))
    q = quarter.astype(jnp.int32)
    odd = (q & 1) == 1
    s = jnp.where(odd, cosine, sine)
    c = jnp.where(odd, sine, cosine)
    s = jnp.where((q & 2) == 2, -s, s)
    c = jnp.where(((q + 1) & 2) == 2, -c, c)
    return s, c


def band(distance, second):
    taps = SECOND_TERMS[1:] if second else FIRST_TERMS
    out = jnp.zeros(distance.shape, jnp.float32)
    for offset in range(1, REACH + 1):
        weight = taps[offset - 1] / taps[0]
        out = jnp.where(distance == offset, weight, out)
        out = jnp.where(distance == -offset, weight if second else -weight, out)
    return out


def iota(shape, dim):
    return lax.broadcasted_iota(jnp.int32, shape, dim)


def dot(a, b):
    return jnp.dot(a, b, preferred_element_type=jnp.float32)


def kernel(
    n,
    wav,
    courant,
    epsilon,
    delta,
    tilt,
    loc,
    counts,
    angle,
    out,
    state,
    c_in,
    e_in,
    d_in,
    t_in,
    ext1,
    ext2,
    edges,
    halos,
    ca,
    cb,
    cd,
    ce,
    cr,
    zmat,
    x2mat,
    x1mat,
    x2edge,
    x1edge,
    step_c,
    step_s,
    slant,
    cos1,
    sin1,
    cos2,
    sin2,
    yre,
    yim,
    img,
    gath,
    in_sem,
    halo_send,
    halo_recv,
    ag_send,
    ag_recv,
):
    me = lax.axis_index("slab")
    _, _, shots, rows, cols = wav.shape
    patches = cols // rows
    bins = rows // 2
    angles = angle.shape[0]
    pairs = 2 * shots
    group = 2 * shots * patches
    half = group // 2
    block = out.shape[0]
    chunks = bins * angles // 128
    split = 8

    def load(j, src, dst):
        copy = pltpu.make_async_copy(src, dst, in_sem.at[j])
        copy.start()
        return copy

    def fields(i, first):
        f, s = i // shots, i % shots
        at = (f, pl.ds(first, 2), s)
        return load(4 + 2 * i + first // 2, wav.at[at], state.at[at])

    now = [fields(i, 0) for i in range(pairs)]
    coefs = [
        load(j, src, dst)
        for j, (src, dst) in enumerate(
            ((tilt, t_in), (epsilon, e_in), (delta, d_in), (courant, c_in))
        )
    ]
    before = [fields(i, 2) for i in range(pairs)]

    halos[...] = jnp.zeros(halos.shape, jnp.bfloat16)

    barrier = pltpu.get_barrier_semaphore()
    for d in range(1, n):
        pl.semaphore_signal(
            barrier, inc=1, device_id={"slab": lax.rem(me + d, n)}, device_id_type=MESH
        )

    tall = rows + 2 * PAD
    col = iota((rows, tall), 1)
    for w in range(2):
        source = jnp.where(col < PAD, col - 8 * w - 8, col - PAD)
        source = jnp.where(col >= PAD + rows, source - 8 * w, source)
        strange = (col < PAD) & (col // 8 != w)
        strange |= (col >= PAD + rows) & ((col - PAD - rows) // 8 != w)
        reach = jnp.where(strange, rows, source - iota((rows, tall), 0))
        zmat[w, 0:rows] = band(reach, True).astype(jnp.bfloat16)
        zmat[w, rows:] = band(reach, False).astype(jnp.bfloat16)
    apart = iota((LANES, LANES), 0) - iota((LANES, LANES), 1)
    for mat, edge, second in ((x2mat, x2edge, True), (x1mat, x1edge, False)):
        here = band(apart, second).astype(jnp.bfloat16)
        left = band(apart - LANES, second).astype(jnp.bfloat16)
        right = band(apart + LANES, second).astype(jnp.bfloat16)
        mat[0:LANES, 0:LANES] = here
        mat[LANES:, LANES:] = here
        mat[0:LANES, LANES:] = left
        mat[LANES:, 0:LANES] = right
        edge[0] = left
        edge[1] = right

    lanes = 2 * angles
    modulus = 16 * rows
    lane = iota((1, lanes), 1)
    slope = jnp.zeros((1, lanes), jnp.int32)
    for a in range(angles):
        slope = jnp.where(lane % angles == a, angle[a], slope)
    step = slope * iota((rows, lanes), 0)
    scale = 1.0 / math.sqrt(rows)

    def phase(j):
        j = jnp.bitwise_and(j, modulus - 1)
        return sincos_turns(j.astype(jnp.float32) * (1.0 / modulus))

    one = jnp.ones((rows, lanes), jnp.float32)
    sin1[0], cos1[0] = 0.0 * one, one
    fine_s, fine_c = phase(step)
    coarse_s, coarse_c = phase(split * step)
    first_half = iota((rows, lanes), 1) < angles
    sin2[0] = jnp.where(first_half, 0.0, scale)
    cos2[0] = jnp.where(first_half, scale, 0.0)
    sin1[1], cos1[1] = coarse_s, coarse_c
    sin2[1] = jnp.where(first_half, fine_s, fine_c) * scale
    cos2[1] = jnp.where(first_half, fine_c, -fine_s) * scale

    def phases(k, carry):
        c, s = cos1[k], sin1[k]
        cos1[k + 1] = c * cos1[1] - s * sin1[1]
        sin1[k + 1] = s * cos1[1] + c * sin1[1]
        c, s = cos2[k], sin2[k]
        fc, fs = step_c[...], step_s[...]
        cos2[k + 1] = c * fc - s * fs
        sin2[k + 1] = s * fc + c * fs
        return carry

    step_c[...] = fine_c
    step_s[...] = fine_s
    lax.fori_loop(1, split - 1, phases, 0)

    pl.semaphore_wait(barrier, n - 1)

    up = jnp.maximum(me - 1, 0)
    down = jnp.minimum(me + 1, n - 1)

    def halo(step, i, upward):
        way = 0 if upward else 1
        return pltpu.make_async_remote_copy(
            src_ref=edges.at[step, i, way],
            dst_ref=halos.at[step, i, way],
            send_sem=halo_send.at[step, way, i],
            recv_sem=halo_recv.at[step, way, i],
            device_id={"slab": up if upward else down},
            device_id_type=MESH,
        )

    def put_edges(step, i, p, q):
        for way, cut in ((0, slice(0, 8)), (1, slice(rows - 8, rows))):
            both = jnp.concatenate([p[cut], q[cut]], axis=0)
            edges[step, i, way] = both.astype(jnp.bfloat16)

    def send(step, i):
        @pl.when(me > 0)
        def _():
            halo(step, i, True).start()

        @pl.when(me < n - 1)
        def _():
            halo(step, i, False).start()

    def receive(step, i):
        @pl.when(me > 0)
        def _():
            halo(step, i, False).wait_recv()

        @pl.when(me < n - 1)
        def _():
            halo(step, i, True).wait_recv()

    def finish(step, i):
        @pl.when(me > 0)
        def _():
            halo(step, i, True).wait_send()

        @pl.when(me < n - 1)
        def _():
            halo(step, i, False).wait_send()

    def convert(i):
        f, s = i // shots, i % shots
        for w in range(2):
            ext1[2 * i + w] = state[f, w, s].astype(jnp.bfloat16)

    for i in range(pairs):
        f, s = i // shots, i % shots
        now[i].wait()
        put_edges(0, i, state[f, 0, s], state[f, 1, s])
        send(0, i)
    for i in range(pairs):
        convert(i)

    for copy in coefs:
        copy.wait()
    sine, cosine = sincos_turns(t_in[...] * (1.0 / math.pi))
    second_scale, first_scale = SECOND_TERMS[1], FIRST_TERMS[0]
    ca[...] = (0.5 * second_scale) * (1.0 - cosine)
    cb[...] = (0.5 * second_scale) * (1.0 + cosine)
    cd[...] = (first_scale * first_scale) * sine
    ce[...] = c_in[...] * (1.0 + 2.0 * e_in[...])
    cr[...] = c_in[...] * jnp.sqrt(1.0 + 2.0 * d_in[...])

    def slants(k1, carry):
        for k2 in range(split):
            k = k1 * split + k2
            for r in range(0, rows, 32):
                at = pl.ds(r, 32)
                c1, s1 = cos1[k1, at], sin1[k1, at]
                c2, s2 = cos2[k2, at], sin2[k2, at]
                slant[k, at, :] = (c1 * c2 - s1 * s2).astype(jnp.bfloat16)
                slant[k, pl.ds(rows + r, 32), :] = (s1 * c2 + c1 * s2).astype(jnp.bfloat16)
        return carry

    lax.fori_loop(0, bins // split, slants, 0)

    centre = SECOND_TERMS[0]

    wide = 2 * LANES

    def along_x(x, mat, edge):
        pieces = []
        for c in range(0, cols, wide):
            y = dot(x[:, c : c + wide], mat[...])
            low, top = y[:, :LANES], y[:, LANES:]
            if c > 0:
                low = low + dot(x[:, c - LANES : c], edge[0])
            if c + wide < cols:
                top = top + dot(x[:, c + wide : c + wide + LANES], edge[1])
            pieces += [low, top]
        return jnp.concatenate(pieces, axis=1)

    def terms(ext, step, i, p, q):
        above, below = halos[step, i, 1], halos[step, i, 0]
        zp = dot(zmat[0], jnp.concatenate([above, ext[2 * i], below], axis=0))
        zq = dot(zmat[1], jnp.concatenate([above, ext[2 * i + 1], below], axis=0))
        both = ext[2 * i : 2 * i + 2].reshape(2 * rows, cols)
        xx = along_x(both, x2mat, x2edge)
        mixed = jnp.concatenate([zp[rows:], zq[rows:]], axis=0).astype(jnp.bfloat16)
        xz = along_x(mixed, x1mat, x1edge)
        a, b, d = ca[...], cb[...], cd[...]
        across = b * xx[:rows] + a * zp[:rows] - d * xz[:rows] + centre * p
        along = a * xx[rows:] + b * zq[:rows] + d * xz[rows:] + centre * q
        return across, along

    for i in range(pairs):
        f, s = i // shots, i % shots
        before[i].wait()
        receive(0, i)
        p0, q0 = state[f, 0, s], state[f, 1, s]
        across, along = terms(ext1, 0, i, p0, q0)
        p = 2.0 * p0 - state[f, 2, s] + ce[...] * across + cr[...] * along
        q = 2.0 * q0 - state[f, 3, s] + cr[...] * across + c_in[...] * along
        state[f, 2, s] = p
        state[f, 3, s] = q
        put_edges(1, i, p, q)
        ext2[2 * i] = p.astype(jnp.bfloat16)
        ext2[2 * i + 1] = q.astype(jnp.bfloat16)
        send(1, i)

    kk = iota((rows, rows), 0)
    zz_ = iota((rows, rows), 1)
    turns = jnp.bitwise_and(jnp.where(kk >= bins, kk - bins, kk) * zz_, rows - 1)
    s_t, c_t = sincos_turns(turns.astype(jnp.float32) * (1.0 / rows))
    table = jnp.where(kk >= bins, -s_t, c_t) * scale
    table_hi = table.astype(jnp.bfloat16)
    table_lo = (table - table_hi.astype(jnp.float32)).astype(jnp.bfloat16)
    table = jnp.concatenate([table_hi, table_hi], axis=1)

    for i in range(pairs):
        f, s = i // shots, i % shots
        receive(1, i)
        p1 = state[f, 2, s]
        across, along = terms(ext2, 1, i, p1, state[f, 3, s])
        p = 2.0 * p1 - state[f, 0, s] + ce[...] * across + cr[...] * along
        p_hi = p.astype(jnp.bfloat16)
        p_lo = (p - p_hi.astype(jnp.float32)).astype(jnp.bfloat16)
        spectrum = dot(table, jnp.concatenate([p_hi, p_lo], axis=0)) + dot(table_lo, p_hi)
        for m in range(patches):
            part = spectrum[:, m * rows : (m + 1) * rows]
            slot = i * patches + m
            yre[pl.ds(slot, bins, stride=group), :] = part[:bins]
            yim[pl.ds(slot, bins, stride=group), :] = part[bins:]

    def stack(k):
        at = pl.ds(pl.multiple_of(k * group, group), group)
        data = jnp.concatenate([yre[at, :], yim[at, :]], axis=1)
        st = dot(data.astype(jnp.bfloat16), slant[k])
        prod = st[:half] * st[half:]
        total = prod[:patches]
        for shot in range(1, shots):
            total = total + prod[shot * patches : (shot + 1) * patches]
        return total

    side = iota((patches, lanes), 1) < angles
    unroll = 4

    def images(j, carry):
        for v in range(unroll):
            t = j * unroll + v
            even, odd = stack(2 * t), stack(2 * t + 1)
            keep = jnp.where(side, even, odd)
            give = jnp.where(side, odd, even)
            img[pl.ds(t, patches, stride=chunks), :] = keep + pltpu.roll(give, angles, 1)
        return carry

    live = iota((patches, chunks // 2, lanes), 0) < counts[me]

    def finish_half(w):
        per = chunks // (2 * unroll)
        lax.fori_loop(w * per, (w + 1) * per, images, 0)
        own = jnp.where(live, img[...].reshape(patches, chunks, lanes)[:, w * (chunks // 2) : (w + 1) * (chunks // 2)], 0.0)
        gath[pl.ds(me * patches, patches), w] = own.astype(jnp.bfloat16)

    high = n // 4
    h, m, l = me // 4, (me // 2) % 2, me % 2
    sent = []

    def partner(d, back):
        if high & (high - 1):
            return lax.rem(h + (high - d if back else d), high)
        a, bit = h, 1
        while bit < high:
            if d & bit:
                a = a + bit - 2 * bit * ((a // bit) % 2)
            bit *= 2
        return a

    def ident(a, b, c):
        return a * 4 + b * 2 + c

    def pass_on(b, w, target):
        at = gath.at[pl.ds(b * patches, patches), w]
        copy = pltpu.make_async_remote_copy(
            src_ref=at,
            dst_ref=at,
            send_sem=ag_send.at[len(sent)],
            recv_sem=ag_recv.at[w, b],
            device_id={"slab": target},
            device_id_type=MESH,
        )
        copy.start()
        sent.append(copy)

    mid, low = ident(h, 1 - m, l), ident(h, m, 1 - l)

    def arrive(b, w):
        at = gath.at[pl.ds(b * patches, patches), w]
        pltpu.make_async_remote_copy(
            src_ref=at,
            dst_ref=at,
            send_sem=ag_send.at[0],
            recv_sem=ag_recv.at[w, b],
            device_id={"slab": low},
            device_id_type=MESH,
        ).wait_recv()

    for w in range(2):
        finish_half(w)
        pass_on(me, w, mid)
        for d in range(1, high):
            pass_on(me, w, ident(partner(d, False), m, l))
        pass_on(me, w, low)
    for w in range(2):
        b = ident(h, 1 - m, l)
        arrive(b, w)
        pass_on(b, w, low)
        for d in range(1, high):
            a = partner(d, True)
            b = ident(a, m, l)
            arrive(b, w)
            pass_on(b, w, mid)
            pass_on(b, w, low)
    for w in range(2):
        for d in range(1, high):
            b = ident(partner(d, True), 1 - m, l)
            arrive(b, w)
            pass_on(b, w, low)
    for w in range(2):
        for d in range(high):
            a = partner(d, True)
            arrive(ident(a, m, 1 - l), w)
            arrive(ident(a, 1 - m, 1 - l), w)

    for g in range(block):
        out[g] = gath[loc[me * block + g]].astype(jnp.float32).reshape(chunks, lanes)

    for copy in sent:
        copy.wait_send()
    for i in range(pairs):
        finish(0, i)
        finish(1, i)


def per_device(
    n, wavefields, courant, epsilon, anisotropy_delta, tilt_angle, loc_patch, slab_counts, angle_table
):
    _, _, shots, rows, cols = wavefields.shape
    patches = cols // rows
    bins = rows // 2
    angles = angle_table.shape[0]
    block = loc_patch.shape[0] // n
    chunks = bins * angles // 128
    pairs = 2 * shots
    group = pairs * patches
    high = n // 4
    f32, bf16 = jnp.float32, jnp.bfloat16
    vm = pltpu.VMEM
    plane = vm((rows, cols), f32)
    table = vm((8, rows, 2 * angles), f32)
    ext = vm((2 * pairs, rows, cols), bf16)
    rims = vm((2, pairs, 2, PAD, cols), bf16)
    hbm = pl.BlockSpec(memory_space=pltpu.HBM)
    smem = pl.BlockSpec(memory_space=pltpu.SMEM)
    result = pl.pallas_call(
        functools.partial(kernel, n),
        out_shape=jax.ShapeDtypeStruct((block, chunks, 128), f32),
        in_specs=[hbm] * 5 + [smem] * 3,
        out_specs=pl.BlockSpec(memory_space=pltpu.VMEM),
        scratch_shapes=[
            vm(wavefields.shape, f32),
            plane, plane, plane, plane,
            ext, ext, rims, rims,
            plane, plane, plane, plane, plane,
            vm((2, 2 * rows, rows + 2 * PAD), bf16),
            vm((2 * LANES, 2 * LANES), bf16),
            vm((2 * LANES, 2 * LANES), bf16),
            vm((2, LANES, LANES), bf16),
            vm((2, LANES, LANES), bf16),
            vm((rows, 2 * angles), f32),
            vm((rows, 2 * angles), f32),
            vm((bins, 2 * rows, 2 * angles), bf16),
            table, table, table, table,
            vm((bins * group, rows), f32),
            vm((bins * group, rows), f32),
            vm((patches * chunks, 2 * angles), f32),
            vm((n * patches, 2, chunks // 2, 2 * angles), bf16),
            pltpu.SemaphoreType.DMA((4 + 2 * pairs,)),
            pltpu.SemaphoreType.DMA((2, 2, pairs)),
            pltpu.SemaphoreType.DMA((2, 2, pairs)),
            pltpu.SemaphoreType.DMA((8 * high,)),
            pltpu.SemaphoreType.DMA((2, n)),
        ],
        compiler_params=pltpu.CompilerParams(
            collective_id=0, has_side_effects=True, vmem_limit_bytes=60 * 1024 * 1024
        ),
        name="imaging",
    )(wavefields, courant, epsilon, anisotropy_delta, tilt_angle, loc_patch, slab_counts, angle_table)
    return result.reshape(block, chunks * 128)


def solution(mesh):
    return jax.shard_map(
        functools.partial(per_device, mesh.shape["slab"]),
        mesh=mesh,
        in_specs=(
            P(None, None, "groups", "slab", None),
            P("slab", None),
            P("slab", None),
            P("slab", None),
            P("slab", None),
            P(),
            P(),
            P(),
        ),
        out_specs=P(("groups", "slab"), None),
        check_vma=False,
    )
```
